256 devices in a mesh: wide: 128 (over y_lo, z, x, core), lev: 2 (over y_hi).
Axes of the slice: x: 4, y: 4 (y_hi: 2, y_lo: 2; y = y_hi * 2 + y_lo), z: 8, core: 2. Of those that a mesh axis runs over, the one named last changes fastest.
Arguments:
- member_control: float32 [128, 128, 128], P('wide'), may hold values from -6 to 6
- static_control: float32 [8, 1024, 1024], P('lev', 'wide'), may hold values from -6 to 6
- perturbations: bfloat16 [128, 8, 1024, 1024], P(None, 'lev', 'wide'), may hold values from -6 to 6
- innovation: float32 [8, 1024, 1024], P('lev', 'wide'), may hold values from -9 to 9
- diffusivity: float32 [8, 1024, 1024], P('lev', 'wide'), may hold values from 0.05 to 0.15
- rows_factor: float32 [128, 128], replicated, may hold values from -0.5 to 0.5
- column_factor: float32 [128, 128], replicated, may hold values from -0.5 to 0.5
- ocean_mask: int32 [1024, 1024], P('wide'), may hold values 0 or 1
- huber_blocks: int32 [8, 128, 128], P('lev', 'wide'), may hold values 0 or 1
- fold_map: int32 [1024], replicated, may hold values from 0 to 1023, as said below
Outputs:
- increment: float32 [8, 1024, 1024], P('lev', 'wide')
- member_gradient: float32 [128, 128, 128], P('wide')
- static_gradient: float32 [8, 1024, 1024], P('lev', 'wide')
The draws below stay inside these ranges and needn't reach their ends.
Inputs may be any that keep to these rules, and one draw needn't show every extreme that they name: fold_map[fold_map[j]] = j and fold_map[j] != j for every column j.
All inputs are finite; a program needn't handle non-finite values. No bound on the sum of `ocean_mask` or of `huber_blocks` on one device may be relied on, other than what follows from the above.
Results may differ from the reference program's by a relative error of at most 0.0003.
Values sent between devices are 32-bit elements; how exact they have to be, the bound alone decides.
A program may use at most 64 MiB of HBM per device.

```python
import jax
import jax.numpy as jnp
from jax import lax

CW = 128
REFINE = 8
LEV = 8
STEPS = 3
MEMBERS = 128
CH = 128
FH = 1024
FW = 1024


def draw_fold_map(key, part):
    shuffled = jax.random.permutation(jax.random.fold_in(key, 7), FW).astype(jnp.int32)
    first_half = shuffled[0::2]
    second = shuffled[1::2]
    partner = jnp.zeros((FW,), jnp.int32)
    partner = partner.at[first_half].set(second).at[second].set(first_half)
    return partner


def touch_ends(entries, key, low, largest):
    extent = entries.shape
    index_at = [jax.random.randint(jax.random.fold_in(key, axis), (), 0, extent[axis]) for axis in range(len(extent))]
    entries = entries.at[tuple(index_at)].set(low)
    longest = extent.index(max(extent))
    index_at[longest] = (index_at[longest] + 1) % extent[longest]
    return entries.at[tuple(index_at)].set(largest)


def levels(key, extent, cuts, smallest, largest):
    level, own = 1.0, jax.random.fold_in(key, 6)
    for axis_at, shards_of in cuts:
        steps = jnp.exp(jax.random.uniform(jax.random.fold_in(own, axis_at), (shards_of,), jnp.float32, smallest / len(cuts), largest / len(cuts)))
        level = level * jnp.repeat(steps, extent[axis_at] // shards_of).reshape([-1 if axis == axis_at else 1 for axis in range(len(extent))])
    return level


def scatter_about(stream_key, dims, spread, reach, shards=(), kind=jnp.bfloat16):
    level = levels(stream_key, dims, shards, -0.22, 0.18) if shards else 1.0
    entries = jax.random.normal(stream_key, dims, jnp.float32) * spread * level
    return jnp.minimum(jnp.maximum(entries, -reach), reach).astype(kind)


def setup_inputs(seed: int = 0) -> dict:
    keys = jax.random.split(jax.random.key(seed), 11)
    member_control = scatter_about(keys[0], (MEMBERS, CH, CW), 1.0, 6.0, ((0, 128),), jnp.float32)
    static_control = scatter_about(keys[1], (LEV, FH, FW), 1.0, 6.0, ((0, 2), (1, 128)), jnp.float32)
    perturbations = scatter_about(keys[2], (MEMBERS, LEV, FH, FW), 1.0, 6.0, ((1, 2), (2, 128)))
    innovation = scatter_about(keys[3], (LEV, FH, FW), 1.5, 9.0, ((0, 2), (1, 128)), jnp.float32)
    diffusivity = jnp.clip(0.05 + 0.10000001 * jax.random.uniform(keys[4], (LEV, FH, FW), jnp.float32) ** levels(keys[4], (LEV, FH, FW), ((0, 2), (1, 128)), -0.2, 0.2), 0.05, 0.15)
    rows_factor = scatter_about(keys[5], (CH, CH), CH ** -0.5, 0.5, (), jnp.float32)
    column_factor = scatter_about(keys[6], (CW, CW), CW ** -0.5, 0.5, (), jnp.float32)
    ocean_mask = touch_ends((jax.random.randint(keys[7], (FH, FW), 0, 5) < 4).astype(jnp.int32), jax.random.fold_in(keys[7], 1), 0, 1)
    huber_blocks = touch_ends((jax.random.randint(keys[8], (LEV, CH, CW), 0, 2) < 1).astype(jnp.int32), jax.random.fold_in(keys[8], 1), 0, 1)
    fold_map = draw_fold_map(jax.random.fold_in(keys[10], 71), 0)
    return dict(member_control=member_control, static_control=static_control, perturbations=perturbations, innovation=innovation, diffusivity=diffusivity, rows_factor=rows_factor, column_factor=column_factor, ocean_mask=ocean_mask, huber_blocks=huber_blocks, fold_map=fold_map)


HUBER_EDGE = 1.0
VERTICAL_WEIGHT = 0.5
PRECISE = lax.Precision.HIGHEST

def smooth_fields(values, rows_factor, column_factor):
    left_done = jnp.einsum('ij,mjk->mik', rows_factor, values, precision=PRECISE)
    return jnp.einsum('mik,kl->mil', left_done, column_factor, precision=PRECISE)

def smooth_adjoint(values, rows_factor, column_factor):
    left_done = jnp.einsum('ji,mjk->mik', rows_factor, values, precision=PRECISE)
    return jnp.einsum('mik,lk->mil', left_done, column_factor, precision=PRECISE)

def interpolate(extended, refine):
    fraction = jnp.arange(refine, dtype=jnp.float32) / refine
    below_row = extended[..., :-1, None, :]
    above_row = extended[..., 1:, None, :]
    row_terms = below_row * (1.0 - fraction)[:, None] + above_row * fraction[:, None]
    dims_of = row_terms.shape
    row_terms = row_terms.reshape(dims_of[:-3] + (dims_of[-3] * refine, dims_of[-1]))
    wrapped = jnp.roll(row_terms, -1, axis=-1)
    col_terms = row_terms[..., None] * (1.0 - fraction) + wrapped[..., None] * fraction
    return col_terms.reshape(row_terms.shape[:-1] + (row_terms.shape[-1] * refine,))

def interpolate_adjoint(fine_field, refine):
    fraction = jnp.arange(refine, dtype=jnp.float32) / refine
    dims_of = fine_field.shape
    col_terms = fine_field.reshape(dims_of[:-1] + (dims_of[-1] // refine, refine))
    coarse_cols = lax.optimization_barrier(jnp.sum(col_terms * (1.0 - fraction), axis=-1)) + jnp.roll(lax.optimization_barrier(jnp.sum(col_terms * fraction, axis=-1)), 1, axis=-1)
    row_terms = coarse_cols.reshape(dims_of[:-2] + (dims_of[-2] // refine, refine, dims_of[-1] // refine))
    below_part = lax.optimization_barrier(jnp.sum(row_terms * (1.0 - fraction)[:, None], axis=-2))
    above_part = lax.optimization_barrier(jnp.sum(row_terms * fraction[:, None], axis=-2))
    zero_row = jnp.zeros_like(below_part[..., :1, :])
    return jnp.concatenate([below_part, zero_row], axis=-2) + jnp.concatenate([zero_row, above_part], axis=-2)

def diffuse(values, diffusivity, fold_map):
    root_kappa = jnp.sqrt(diffusivity)
    for _ in range(STEPS):
        scaled = root_kappa * values
        padded = jnp.pad(scaled, ((1, 1), (1, 1), (0, 0)))
        folded = jnp.take(scaled[:, -1, :], fold_map, axis=1)
        padded = padded.at[1:-1, -1, :].set(folded)
        across = padded[1:-1, 2:, :] + padded[1:-1, :-2, :] + jnp.roll(scaled, 1, axis=2) + jnp.roll(scaled, -1, axis=2) - 4.0 * scaled
        vertical = padded[2:, 1:-1, :] + padded[:-2, 1:-1, :] - 2.0 * scaled
        values = values + root_kappa * (across + VERTICAL_WEIGHT * vertical)
    return values

def huber_weigh(increment, innovation, ocean_cells, huber_blocks):
    misfit = increment - innovation
    expanded = jnp.repeat(jnp.repeat(huber_blocks, REFINE, axis=1), REFINE, axis=2)
    weight = jnp.where(expanded == 1, HUBER_EDGE / jnp.maximum(jnp.abs(misfit), HUBER_EDGE), 1.0)
    return ocean_cells * weight * misfit

def reference(member_control, static_control, perturbations, innovation, diffusivity, rows_factor, column_factor, ocean_mask, huber_blocks, fold_map):
    member_scale = (MEMBERS - 1) ** (-0.5)
    smoothed = smooth_fields(member_control, rows_factor, column_factor)
    extended = jnp.concatenate([smoothed, smoothed[:, -1:, :]], axis=1)

    def add_member(running, member_pair):
        ext_one, pert_one = member_pair
        fine_field = interpolate(ext_one, REFINE)
        return (running + fine_field[None] * pert_one, None)
    initial = jnp.zeros((LEV, FH, FW), jnp.float32)
    ensemble, _ = lax.scan(add_member, initial, (extended, perturbations))
    ocean_cells = ocean_mask.astype(jnp.float32)
    increment = ocean_cells * (member_scale * ensemble + diffuse(static_control, diffusivity, fold_map))
    weighted = huber_weigh(increment, innovation, ocean_cells, huber_blocks)
    static_gradient = static_control + diffuse(weighted, diffusivity, fold_map)

    def member_terms(pert_one):
        fine_terms = lax.optimization_barrier(jnp.sum(pert_one * weighted, axis=0)) * member_scale
        return interpolate_adjoint(fine_terms, REFINE)
    ext_grad = lax.map(member_terms, perturbations)
    smooth_grad = ext_grad[:, :-1, :].at[:, -1, :].add(ext_grad[:, -1, :])
    member_gradient = member_control + smooth_adjoint(smooth_grad, rows_factor, column_factor)
    return (increment, member_gradient, static_gradient)
```

```python
import functools

import jax
import jax.numpy as jnp
from jax import lax
from jax.experimental import pallas as pl
from jax.experimental.pallas import tpu as pltpu
from jax.sharding import PartitionSpec as P

STEPS = 3
WIDE = 128
GROUP = 16
GROUPS = WIDE // GROUP
LEVELS = 4
TILES = 8
F32 = jnp.float32
BF16 = jnp.bfloat16
MESH = pl.DeviceIdType.MESH
PRECISE = lax.Precision.HIGHEST
SCALE = 127.0 ** (-0.5)
OWN = LEVELS * 64
HALO = STEPS * 64
ALL_ROWS = (8 + 2 * STEPS) * 64


def rows_at(start, size, step=1):
    if step == 1:
        return pl.ds(pl.multiple_of(start, 8), size)
    return pl.ds(start, size, stride=step)


def kernel(
    mc_hbm, sc_hbm, pert_hbm, inn_hbm, dif_hbm, rf_hbm, cf_hbm, mask_hbm, hub_hbm, fold_hbm,
    inc_hbm, mg_hbm, sg_hbm,
    pert, mc, cf, r2, win, ext, bb, sb, nat_s, nat_k, nat_w, inn, mask, hub, fold,
    v_s, v_w, kap, s_buf, tmp, ww, wt, lhs, fbuf, gbuf, ens, wsc, hubx, incb, sgb, mgb,
    load_sem, out_sem, fwd_send, fwd_recv, bwd_send, bwd_recv, lev_send, lev_recv, row_send, row_recv,
):
    w = lax.axis_index("wide")
    lev = lax.axis_index("lev")
    group, place = w // GROUP, w % GROUP
    right, left = (w + 1) % WIDE, (w + WIDE - 1) % WIDE
    own0 = pl.multiple_of(lev * OWN, OWN)

    def remote(src, dst, send, recv, wide=None, level=None):
        target = {"wide": w if wide is None else wide, "lev": lev if level is None else level}
        return pltpu.make_async_remote_copy(
            src_ref=src, dst_ref=dst, send_sem=send, recv_sem=recv, device_id=target, device_id_type=MESH
        )

    def wait_bytes(ref, sem):
        pltpu.make_async_copy(ref, ref, sem).wait()

    barrier = pltpu.get_barrier_semaphore()

    def tell(i, _):
        pl.semaphore_signal(barrier, inc=1, device_id={"wide": (w + i) % WIDE, "lev": lev}, device_id_type=MESH)
        return _

    lax.fori_loop(1, WIDE, tell, 0)
    pl.semaphore_signal(barrier, inc=1, device_id={"wide": w, "lev": 1 - lev}, device_id_type=MESH)

    loads = [
        (mc_hbm, mc), (cf_hbm, cf), (rf_hbm, tmp.at[pl.ds(0, 128)]),
        (sc_hbm, nat_s.at[pl.ds(own0, OWN)]), (dif_hbm, nat_k.at[pl.ds(own0, OWN)]),
        (pert_hbm, pert), (inn_hbm, inn), (mask_hbm, mask), (hub_hbm, hub.at[pl.ds(0, LEVELS)]), (fold_hbm, fold),
    ]
    loads = [pltpu.make_async_copy(src, dst, load_sem.at[i]) for i, (src, dst) in enumerate(loads)]
    for load in loads:
        load.start()

    j = lax.broadcasted_iota(jnp.int32, (WIDE, 1024), 0)
    x = lax.broadcasted_iota(jnp.int32, (WIDE, 1024), 1)
    part = (x % 8).astype(F32) * 0.125
    weights = jnp.where(x // 8 == j, 1.0 - part, 0.0) + jnp.where((x // 8 + 1) % WIDE == j, part, 0.0)
    ww[0:128] = weights.astype(BF16)
    ww[128:256] = weights.astype(BF16)
    x = lax.broadcasted_iota(jnp.int32, (1024, WIDE), 0)
    j = lax.broadcasted_iota(jnp.int32, (1024, WIDE), 1)
    part = (x % 8).astype(F32) * 0.125
    weights = jnp.where(x // 8 == j, 1.0 - part, 0.0) + jnp.where((x // 8 + 1) % WIDE == j, part, 0.0)
    wt[...] = weights.astype(BF16)

    for i in range(3):
        loads[i].wait()
    r2[pl.ds(0, 128, stride=2), :] = tmp[0:128]
    r2[pl.ds(1, 128, stride=2), :] = jnp.concatenate([tmp[1:128], tmp[127:128]], axis=0)
    columns_done = jnp.dot(mc[...], cf[...], precision=PRECISE, preferred_element_type=F32)
    win[...] = jnp.dot(r2[...], columns_done, precision=PRECISE, preferred_element_type=F32)

    pl.semaphore_wait(barrier, WIDE)

    def offset_of(n):
        return 4 + (1 - 2 * (n % 2)) * ((n + 1) // 2)

    def send_window(n, _):
        i = offset_of(n // GROUP)
        to = ((group + i) % GROUPS) * GROUP + (place + n % GROUP) % GROUP
        remote(win.at[pl.ds(2 * to, 2)], ext.at[pl.ds(2 * w, 2)], fwd_send, fwd_recv.at[i], wide=to).start()
        return _

    lax.fori_loop(0, 7 * GROUP, send_window, 0)
    lax.fori_loop(7 * GROUP + 1, 8 * GROUP, send_window, 0)
    pltpu.make_async_copy(win.at[pl.ds(2 * w, 2)], ext.at[pl.ds(2 * w, 2)], fwd_recv.at[0]).start()

    for i in (3, 4):
        loads[i].wait()
    seen = pl.ds(pl.multiple_of(64 + 192 * lev, 64), 192)
    unseen = pl.ds(pl.multiple_of(448 * (1 - lev), 64), 64)
    lev_copies = [
        remote(nat.at[seen], nat.at[seen], lev_send.at[i], lev_recv.at[i], level=1 - lev)
        for i, nat in enumerate((nat_s, nat_k, nat_w))
    ]
    lev_copies[0].start()
    lev_copies[1].start()
    for nat in (nat_s, nat_k, nat_w):
        nat[unseen, :] = jnp.zeros((64, 128), F32)

    def to_rows(nat, out, change):
        def body(r, _):
            for t in range(TILES):
                out[rows_at((r + STEPS) * 64 + t * 8, 8), :] = change(nat[rows_at(t * 8 + r, 8, 64), :])
            return _

        lax.fori_loop(0, 8, body, 0)

    def to_natural(rows, out):
        def body(r, _):
            for t in range(TILES):
                out[rows_at(t * 8 + r, 8, 64), :] = rows[rows_at((r + STEPS) * 64 + t * 8, 8), :]
            return _

        lax.fori_loop(0, 8, body, 0)

    def row_copies(rows, i):
        down = remote(rows.at[pl.ds(8 * 64, HALO)], rows.at[pl.ds(0, HALO)], row_send.at[i], row_recv.at[i], wide=right)
        up = remote(
            rows.at[pl.ds(3 * 64, HALO)], rows.at[pl.ds(11 * 64, HALO)], row_send.at[i + 1], row_recv.at[i + 1], wide=left
        )
        return [down, up]

    static_rows = row_copies(v_s, 0) + row_copies(kap, 2)
    weighted_rows = row_copies(v_w, 4)

    sublane = lax.broadcasted_iota(jnp.int32, (8, 8, 128), 1)
    lane = lax.broadcasted_iota(jnp.int32, (64, 128), 1)

    def fold_row(row):
        def body(t, _):
            entry = jnp.broadcast_to(fold[pl.ds(t, 1), :], (8, 128))
            at, tile = entry % 128, entry // 128
            total = jnp.zeros((8, 128), F32)
            for u in range(TILES):
                there = jnp.take_along_axis(s_buf[pl.ds(row * 64 + u * 8, 8), :], at, axis=1)
                total = jnp.where(tile == u, there, total)
            here = rows_at((row + 1) * 64 + t * 8, 8)
            s_buf[here, :] = jnp.where(w == WIDE - 1, total, s_buf[here, :])
            return _

        lax.fori_loop(0, TILES, body, 0)

    def diffuse(v):
        for step in range(1, STEPS + 1):
            def scale_row(i, _):
                here = rows_at(i * 64, 64)
                s_buf[here, :] = kap[here, :] * v[here, :]
                return _

            lax.fori_loop(step - 1, 8 + 2 * STEPS + 1 - step, scale_row, 0)
            fold_row(STEPS + 7)

            def update_row(i, _):
                here = rows_at(i * 64, 64)
                s = s_buf[here, :]
                after = pltpu.roll(s, 1, 1)
                before = pltpu.roll(s, 127, 1)
                west = jnp.where(lane == 0, jnp.concatenate([after[56:], after[:56]], axis=0), after)
                east = jnp.where(lane == 127, jnp.concatenate([before[8:], before[:8]], axis=0), before)
                s3 = s.reshape(8, 8, 128)
                below = jnp.where(sublane == 0, 0.0, pltpu.roll(s3, 1, 1)).reshape(64, 128)
                above = jnp.where(sublane == 7, 0.0, pltpu.roll(s3, 7, 1)).reshape(64, 128)
                across = s_buf[rows_at(i * 64 + 64, 64), :] + s_buf[rows_at(i * 64 - 64, 64), :] + west + east
                v[here, :] = v[here, :] + kap[here, :] * (across + 0.5 * (below + above) - 5.0 * s)
                return _

            lax.fori_loop(step, 8 + 2 * STEPS - step, update_row, 0)

    eighth = lax.broadcasted_iota(jnp.int32, (8, 128), 0).astype(F32) * 0.125
    loads[5].wait()
    ens[...] = jnp.zeros((LEVELS, 8, 1024), F32)

    def ensemble_group(n, _):
        i = offset_of(7 - n)
        first = ((group + GROUPS - i) % GROUPS) * GROUP
        wait_bytes(ext.at[pl.ds(0, 2 * GROUP)], fwd_recv.at[i])
        for mm in range(GROUP):
            at = 2 * (first + mm)
            lhs[mm * 8 : mm * 8 + 8] = (
                ext[pl.ds(at, 8, stride=0), :] * (1.0 - eighth) + ext[pl.ds(at + 1, 8, stride=0), :] * eighth
            )
        high = lhs[...].astype(BF16)
        low = (lhs[...] - high.astype(F32)).astype(BF16)
        fbuf[...] = jnp.dot(jnp.concatenate([high, low], axis=1), ww[...], preferred_element_type=F32)

        def member(mm, total):
            fine = fbuf[rows_at(mm * 8, 8), :]
            return tuple(total[l] + fine * pert[first + mm, l].astype(F32) for l in range(LEVELS))

        total = lax.fori_loop(0, GROUP, member, tuple(ens[l] for l in range(LEVELS)), unroll=2)
        for l in range(LEVELS):
            ens[l] = total[l]
        return _

    def halves(n, _):
        return ensemble_group(n, _)

    lax.fori_loop(0, 4, halves, 0)

    lev_copies[0].wait_recv()
    lev_copies[1].wait_recv()
    to_rows(nat_s, v_s, lambda value: value)
    to_rows(nat_k, kap, jnp.sqrt)
    for copy in static_rows:
        copy.start()

    lax.fori_loop(4, 8, halves, 0)

    for copy in static_rows:
        copy.wait()
    loads[9].wait()
    kap[0:HALO] = jnp.where(w == 0, 0.0, kap[0:HALO])
    kap[11 * 64 : ALL_ROWS] = jnp.where(w == WIDE - 1, 0.0, kap[11 * 64 : ALL_ROWS])
    diffuse(v_s)
    to_natural(v_s, tmp)

    for i in (6, 7, 8):
        loads[i].wait()
    j = lax.broadcasted_iota(jnp.int32, (WIDE, 1024), 0)
    x = lax.broadcasted_iota(jnp.int32, (WIDE, 1024), 1)
    spread = jnp.where(x // 8 == j, 1.0, 0.0).astype(BF16)
    blocks = jnp.concatenate([jnp.where(hub[0:LEVELS] == 1, 1.0, 0.0), jnp.zeros((12, 128), F32)], axis=0).astype(BF16)
    hubx[...] = jnp.dot(blocks, spread, preferred_element_type=F32)
    for t in range(TILES):
        columns = slice(t * 128, t * 128 + 128)
        ocean = mask[t * 8 : t * 8 + 8].astype(F32)
        for l in range(LEVELS):
            at = (l * TILES + t) * 8
            there = rows_at(own0 + at, 8)
            inc = ocean * (SCALE * ens[l, :, columns] + tmp[there, :])
            incb[at : at + 8] = inc
            misfit = inc - inn[at : at + 8]
            is_huber = jnp.broadcast_to(hubx[l : l + 1, columns], (8, 128)) > 0.5
            weight = jnp.where(is_huber, 1.0 / jnp.maximum(jnp.abs(misfit), 1.0), 1.0)
            weighted = ocean * weight * misfit
            nat_w[there, :] = weighted
            wsc[l, :, columns] = weighted * SCALE
    lev_copies[2].start()
    inc_out = pltpu.make_async_copy(incb, inc_hbm, out_sem.at[0])
    inc_out.start()

    def adjoint_group(i, first_place):
        first = ((group + i) % GROUPS) * GROUP

        def member(mm, _):
            total = pert[first + mm, 0].astype(F32) * wsc[0]
            for l in range(1, LEVELS):
                total = total + pert[first + mm, l].astype(F32) * wsc[l]
            fbuf[rows_at(mm * 8, 8), :] = total
            return _

        lax.fori_loop(0, GROUP, member, 0, unroll=2)
        high = fbuf[...].astype(BF16)
        low = (fbuf[...] - high.astype(F32)).astype(BF16)
        gbuf[...] = jnp.dot(high, wt[...], preferred_element_type=F32) + jnp.dot(
            low, wt[...], preferred_element_type=F32
        )
        below = gbuf[pl.ds(0, GROUP, stride=8), :]
        above = jnp.zeros((GROUP, 128), F32)
        for r in range(1, 8):
            row = gbuf[pl.ds(r, GROUP, stride=8), :]
            below = below + row * (1.0 - r * 0.125)
            above = above + row * (r * 0.125)
        sb[pl.ds(2 * first, GROUP, stride=2), :] = below
        sb[pl.ds(2 * first + 1, GROUP, stride=2), :] = above

        def send(n, _):
            member_at = first + (place + n) % GROUP
            for k in range(2):
                remote(
                    sb.at[pl.ds(2 * member_at, 2)], bb.at[pl.ds(2 * (lev * WIDE + w), 2)], bwd_send, bwd_recv,
                    wide=member_at, level=(lev + 1 + k) % 2,
                ).start()
            return _

        lax.fori_loop(first_place, GROUP, send, 0)

    def adjoint_far(n, _):
        adjoint_group(offset_of(n), 0)
        return _

    lax.fori_loop(0, 5, adjoint_far, 0)

    lev_copies[2].wait_recv()
    to_rows(nat_w, v_w, lambda value: value)
    for copy in weighted_rows:
        copy.start()

    lax.fori_loop(5, 7, adjoint_far, 0)
    adjoint_group(0, 1)
    mine = pl.ds(2 * w, 2)
    slot = pl.ds(2 * (lev * WIDE + w), 2)
    remote(sb.at[mine], bb.at[slot], bwd_send, bwd_recv, level=1 - lev).start()
    pltpu.make_async_copy(sb.at[mine], bb.at[slot], bwd_recv).start()

    for copy in weighted_rows:
        copy.wait()
    diffuse(v_w)
    to_natural(v_w, tmp)
    sgb[...] = nat_s[pl.ds(own0, OWN), :] + tmp[pl.ds(own0, OWN), :]
    sg_out = pltpu.make_async_copy(sgb, sg_hbm, out_sem.at[1])
    sg_out.start()

    wait_bytes(bb, bwd_recv)
    terms = bb[0:256] + bb[256:512]
    rows_done = lax.dot_general(
        r2[...], terms, (((0,), (0,)), ((), ())), precision=PRECISE, preferred_element_type=F32
    )
    mgb[...] = mc[...] + lax.dot_general(
        rows_done, cf[...], (((1,), (1,)), ((), ())), precision=PRECISE, preferred_element_type=F32
    )
    mg_out = pltpu.make_async_copy(mgb, mg_hbm, out_sem.at[2])
    mg_out.start()

    wait_bytes(ext.at[pl.ds(0, 254)], fwd_send)
    wait_bytes(bb.at[pl.ds(0, 510)], bwd_send)
    for copy in lev_copies:
        copy.wait_send()
    inc_out.wait()
    sg_out.wait()
    mg_out.wait()


def natural(array):
    levels = array.shape[0]
    return array.reshape(levels, 8, TILES, 128).transpose(0, 2, 1, 3).reshape(levels * 64, 128)


def from_natural(array):
    return array.reshape(LEVELS, TILES, 8, 128).transpose(0, 2, 1, 3).reshape(LEVELS, 8, 1024)


def on_device(
    member_control, static_control, perturbations, innovation, diffusivity,
    rows_factor, column_factor, ocean_mask, huber_blocks, fold_map,
):
    hbm = pl.BlockSpec(memory_space=pltpu.HBM)
    dma = pltpu.SemaphoreType.DMA

    def vmem(*shape, dtype=F32):
        return pltpu.VMEM(shape, dtype)

    increment, member_gradient, static_gradient = pl.pallas_call(
        kernel,
        out_shape=(
            jax.ShapeDtypeStruct((OWN, 128), F32),
            jax.ShapeDtypeStruct((128, 128), F32),
            jax.ShapeDtypeStruct((OWN, 128), F32),
        ),
        in_specs=[hbm] * 10,
        out_specs=[hbm] * 3,
        scratch_shapes=[
            vmem(WIDE, LEVELS, 8, 1024, dtype=BF16),
            vmem(128, 128), vmem(128, 128), vmem(256, 128),
            vmem(256, 128), vmem(256, 128), vmem(512, 128), vmem(256, 128),
            vmem(512, 128), vmem(512, 128), vmem(512, 128),
            vmem(OWN, 128), vmem(64, 128, dtype=jnp.int32), vmem(8, 128, dtype=jnp.int32),
            vmem(8, 128, dtype=jnp.int32),
            vmem(ALL_ROWS, 128), vmem(ALL_ROWS, 128), vmem(ALL_ROWS, 128), vmem(ALL_ROWS, 128),
            vmem(512, 128),
            vmem(256, 1024, dtype=BF16), vmem(1024, 128, dtype=BF16),
            vmem(128, 128), vmem(128, 1024), vmem(128, 128),
            vmem(LEVELS, 8, 1024), vmem(LEVELS, 8, 1024), vmem(16, 1024),
            vmem(OWN, 128), vmem(OWN, 128), vmem(128, 128),
            dma((10,)), dma((3,)), dma, dma((8,)), dma, dma, dma((3,)), dma((3,)), dma((6,)), dma((6,)),
        ],
        compiler_params=pltpu.CompilerParams(
            collective_id=0, has_side_effects=True, vmem_limit_bytes=40 << 20
        ),
        name="increment_and_gradients",
    )(
        member_control.reshape(128, 128),
        natural(static_control),
        perturbations,
        natural(innovation),
        natural(diffusivity),
        rows_factor,
        column_factor,
        natural(ocean_mask[None]),
        huber_blocks.reshape(LEVELS, 128),
        fold_map.reshape(8, 128),
    )
    return from_natural(increment), member_gradient[None], from_natural(static_gradient)


def solution(mesh):
    return jax.shard_map(
        on_device,
        mesh=mesh,
        in_specs=(
            P("wide", None, None),
            P("lev", "wide", None),
            P(None, "lev", "wide", None),
            P("lev", "wide", None),
            P("lev", "wide", None),
            P(),
            P(),
            P("wide", None),
            P("lev", "wide", None),
            P(),
        ),
        out_specs=(P("lev", "wide", None), P("wide", None, None), P("lev", "wide", None)),
        check_vma=False,
    )
```

```python
import functools

import jax
import jax.numpy as jnp
from jax import lax
from jax.experimental import pallas as pl
from jax.experimental.pallas import tpu as pltpu
from jax.sharding import PartitionSpec as P

STEPS = 3
WIDE = 128
GROUP = 16
GROUPS = WIDE // GROUP
D_FIRST = True
BEFORE = 5
LEVELS = 4
TILES = 8
F32 = jnp.float32
BF16 = jnp.bfloat16
MESH = pl.DeviceIdType.MESH
PRECISE = lax.Precision.HIGHEST
SCALE = 127.0 ** (-0.5)
OWN = LEVELS * 64
HALO = STEPS * 64
ALL_ROWS = (8 + 2 * STEPS) * 64
DOWN_SIZE = STEPS * LEVELS * 8
PACKED = 2 * DOWN_SIZE + 48


def rows_at(start, size, step=1):
    if step == 1:
        return pl.ds(pl.multiple_of(start, 8), size)
    return pl.ds(start, size, stride=step)


def kernel(
    mc_hbm, sc_hbm, pert_hbm, inn_hbm, dif_hbm, rf_hbm, cf_hbm, mask_hbm, hub_hbm, fold_hbm,
    inc_hbm, mg_hbm, sg_hbm,
    pert, mc, cf, r2, win, ext, bb, sb, nat_s, nat_k, nat_w, inn, mask, hub, fold,
    v_s, v_w, kap, s_a, s_b, tmp, ww, wt, lhs, fbuf, gbuf, ens, wsc, hubx, incb, sgb, mgb,
    pack, pack_w, from_rows, from_rows_w, half, twin, table,
    load_sem, out_sem, fwd_send, fwd_recv, bwd_send, bwd_recv, lev_send, lev_recv, row_send, row_recv, half_send, half_recv,
):
    w = lax.axis_index("wide")
    lev = lax.axis_index("lev")
    group, place = w // GROUP, w % GROUP
    right, left = (w + 1) % WIDE, (w + WIDE - 1) % WIDE
    own0 = pl.multiple_of(lev * OWN, OWN)

    def remote(src, dst, send, recv, wide=None, level=None):
        target = {"wide": w if wide is None else wide, "lev": lev if level is None else level}
        return pltpu.make_async_remote_copy(
            src_ref=src, dst_ref=dst, send_sem=send, recv_sem=recv, device_id=target, device_id_type=MESH
        )

    def wait_bytes(ref, sem):
        pltpu.make_async_copy(ref, ref, sem).wait()

    loads = [
        (mc_hbm, mc), (cf_hbm, cf), (rf_hbm, tmp.at[pl.ds(0, 128)]),
        (sc_hbm, nat_s.at[pl.ds(own0, OWN)]), (dif_hbm, nat_k.at[pl.ds(own0, OWN)]),
        (pert_hbm, pert), (inn_hbm, inn), (mask_hbm, mask), (hub_hbm, hub.at[pl.ds(0, LEVELS)]), (fold_hbm, fold),
    ]
    loads = [pltpu.make_async_copy(src, dst, load_sem.at[i]) for i, (src, dst) in enumerate(loads)]
    for load in loads:
        load.start()

    barrier = pltpu.get_barrier_semaphore()

    def signal(wide, level):
        pl.semaphore_signal(barrier, inc=1, device_id={"wide": wide, "lev": level}, device_id_type=MESH)

    for wide in (w, left, right):
        signal(wide, 1 - lev)

    column = lax.broadcasted_iota(jnp.int32, (8, 1024), 1)
    cell, part = column // 8, (column % 8).astype(F32) * 0.125

    def table_and_signals(n, _):
        j = lax.broadcasted_iota(jnp.int32, (8, 1024), 0) + n * 8
        both = jnp.where(cell == j, 1.0 - part, 0.0) + jnp.where((cell + 1) % WIDE == j, part, 0.0)
        table[rows_at(n * 8, 8), :] = both
        for k in range(8):
            signal((w + n * 8 + k + 1) % WIDE, lev)
        return _

    lax.fori_loop(0, 15, table_and_signals, 0)
    j = lax.broadcasted_iota(jnp.int32, (8, 1024), 0) + 120
    table[120:128] = jnp.where(cell == j, 1.0 - part, 0.0) + jnp.where((cell + 1) % WIDE == j, part, 0.0)
    for k in range(7):
        signal((w + 121 + k) % WIDE, lev)
    weights = table[...].astype(BF16)
    ww[0:128] = weights
    ww[128:256] = weights
    wt[...] = table[...].T.astype(BF16)

    for i in range(3):
        loads[i].wait()
    r2[pl.ds(0, 128, stride=2), :] = tmp[0:128]
    r2[pl.ds(1, 128, stride=2), :] = jnp.concatenate([tmp[1:128], tmp[127:128]], axis=0)
    columns_done = jnp.dot(mc[...], cf[...], precision=PRECISE, preferred_element_type=F32)
    win[...] = jnp.dot(r2[...], columns_done, precision=PRECISE, preferred_element_type=F32)

    near, next_near = 3 * (1 - lev), 2 - lev

    def pack_rows(nat, out, at):
        def row(level, r):
            return nat[pl.ds(own0 + level * 64 + r, 8, stride=8), :]

        for k in range(STEPS):
            for l in range(LEVELS):
                out[pl.ds(at + (k * LEVELS + l) * 8, 8), :] = row(l, 5 + k)
                out[pl.ds(at + DOWN_SIZE + (k * LEVELS + l) * 8, 8), :] = row(l, k)
        for k, (level, r) in enumerate(((near, 7), (near, 6), (next_near, 7), (near, 0), (near, 1), (next_near, 0))):
            out[pl.ds(at + 2 * DOWN_SIZE + k * 8, 8), :] = row(level, r)

    def unpack_rows(got, at, out, change):
        def put(r, level, value):
            out[pl.ds(r * 64 + level, 8, stride=8), :] = change(value)

        for k in range(STEPS):
            for l in range(LEVELS):
                put(k, lev * LEVELS + l, got[pl.ds(at + (k * LEVELS + l) * 8, 8), :])
                put(11 + k, lev * LEVELS + l, got[pl.ds(at + DOWN_SIZE + (k * LEVELS + l) * 8, 8), :])
        theirs, theirs_next = 4 - lev, 5 - 3 * lev
        for k, (r, level) in enumerate(
            ((2, theirs), (1, theirs), (2, theirs_next), (11, theirs), (12, theirs), (11, theirs_next))
        ):
            put(r, level, got[pl.ds(at + 2 * DOWN_SIZE + k * 8, 8), :])

    def row_copies(out, got, at, i):
        parts = (
            (right, lev, 0, DOWN_SIZE), (left, lev, DOWN_SIZE, DOWN_SIZE),
            (right, 1 - lev, 2 * DOWN_SIZE, 24), (left, 1 - lev, 2 * DOWN_SIZE + 24, 24),
        )
        return [
            remote(
                out.at[pl.ds(at + start, size)], got.at[pl.ds(at + start, size)],
                row_send.at[i + k], row_recv.at[i + k], wide=wide, level=level,
            )
            for k, (wide, level, start, size) in enumerate(parts)
        ]

    seen = pl.ds(pl.multiple_of(64 + 192 * lev, 64), 192)
    unseen = pl.ds(pl.multiple_of(448 * (1 - lev), 64), 64)
    lev_copies = [
        remote(nat.at[seen], nat.at[seen], lev_send.at[i], lev_recv.at[i], level=1 - lev)
        for i, nat in enumerate((nat_s, nat_k, nat_w))
    ]
    static_rows = row_copies(pack, from_rows, 0, 0) + row_copies(pack, from_rows, PACKED, 4)
    weighted_rows = row_copies(pack_w, from_rows_w, 0, 8)
    for i in (3, 4):
        loads[i].wait()
    pack_rows(nat_s, pack, 0)
    pack_rows(nat_k, pack, PACKED)
    for nat in (nat_s, nat_k, nat_w):
        nat[unseen, :] = jnp.zeros((64, 128), F32)
    for rows in (v_s, v_w, kap):
        rows[0:HALO] = jnp.zeros((HALO, 128), F32)
        rows[11 * 64 : ALL_ROWS] = jnp.zeros((HALO, 128), F32)

    pl.semaphore_wait(barrier, WIDE + 2)
    lev_copies[0].start()
    lev_copies[1].start()
    for copy in static_rows:
        copy.start()

    def offset_of(n):
        return 4 + (1 - 2 * (n % 2)) * ((n + 1) // 2)

    def send_window(n, _):
        i = offset_of(n // GROUP)
        to = ((group + i) % GROUPS) * GROUP + (place + n % GROUP) % GROUP
        remote(win.at[pl.ds(2 * to, 2)], ext.at[pl.ds(2 * w, 2)], fwd_send, fwd_recv.at[i], wide=to).start()
        return _

    lax.fori_loop(0, 7 * GROUP, send_window, 0)
    lax.fori_loop(7 * GROUP + 1, 8 * GROUP, send_window, 0)
    pltpu.make_async_copy(win.at[pl.ds(2 * w, 2)], ext.at[pl.ds(2 * w, 2)], fwd_recv.at[0]).start()

    def to_rows(nat, out, change):
        def body(r, _):
            for t in range(TILES):
                out[rows_at((r + STEPS) * 64 + t * 8, 8), :] = change(nat[rows_at(t * 8 + r, 8, 64), :])
            return _

        lax.fori_loop(0, 8, body, 0)

    def to_natural(rows, out):
        def body(r, _):
            for t in range(TILES):
                out[rows_at(t * 8 + r, 8, 64), :] = rows[rows_at((r + STEPS) * 64 + t * 8, 8), :]
            return _

        lax.fori_loop(0, 8, body, 0)

    sublane = lax.broadcasted_iota(jnp.int32, (8, 8, 128), 1)
    lane = lax.broadcasted_iota(jnp.int32, (64, 128), 1)

    def fold_row(s_buf):
        def body(t, _):
            entry = jnp.broadcast_to(fold[pl.ds(t, 1), :], (8, 128))
            at, tile = entry % 128, entry // 128
            total = jnp.zeros((8, 128), F32)
            for u in range(TILES):
                there = jnp.take_along_axis(s_buf[pl.ds(10 * 64 + u * 8, 8), :], at, axis=1)
                total = jnp.where(tile == u, there, total)
            here = rows_at(11 * 64 + t * 8, 8)
            s_buf[here, :] = jnp.where(w == WIDE - 1, total, s_buf[here, :])
            return _

        lax.fori_loop(0, TILES, body, 0)

    def diffuse(v):
        def scale_row(i, _):
            here = rows_at(i * 64, 64)
            s_a[here, :] = kap[here, :] * v[here, :]
            return _

        lax.fori_loop(0, 14, scale_row, 0, unroll=2)
        for step in range(1, STEPS + 1):
            s_buf, s_next = (s_a, s_b) if step % 2 else (s_b, s_a)
            fold_row(s_buf)

            def update_row(i, _):
                here = rows_at(i * 64, 64)
                s = s_buf[here, :]
                after = pltpu.roll(s, 1, 1)
                before = pltpu.roll(s, 127, 1)
                west = jnp.where(lane == 0, jnp.concatenate([after[56:], after[:56]], axis=0), after)
                east = jnp.where(lane == 127, jnp.concatenate([before[8:], before[:8]], axis=0), before)
                s3 = s.reshape(8, 8, 128)
                below = jnp.where(sublane == 0, 0.0, pltpu.roll(s3, 1, 1)).reshape(64, 128)
                above = jnp.where(sublane == 7, 0.0, pltpu.roll(s3, 7, 1)).reshape(64, 128)
                across = s_buf[rows_at(i * 64 + 64, 64), :] + s_buf[rows_at(i * 64 - 64, 64), :] + west + east
                new = v[here, :] + kap[here, :] * (across + 0.5 * (below + above) - 5.0 * s)
                v[here, :] = new
                if step < STEPS:
                    s_next[here, :] = kap[here, :] * new
                return _

            lax.fori_loop(step, 14 - step, update_row, 0, unroll=2)

    eighth = lax.broadcasted_iota(jnp.int32, (8, 128), 0).astype(F32) * 0.125
    loads[5].wait()
    ens[...] = jnp.zeros((LEVELS, 8, 1024), F32)

    def ensemble_group(n, _):
        i = offset_of(7 - n)
        first = ((group + GROUPS - i) % GROUPS) * GROUP
        wait_bytes(ext.at[pl.ds(0, 2 * GROUP)], fwd_recv.at[i])
        for mm in range(GROUP):
            at = 2 * (first + mm)
            lhs[mm * 8 : mm * 8 + 8] = (
                ext[pl.ds(at, 8, stride=0), :] * (1.0 - eighth) + ext[pl.ds(at + 1, 8, stride=0), :] * eighth
            )
        high = lhs[...].astype(BF16)
        low = (lhs[...] - high.astype(F32)).astype(BF16)
        fbuf[...] = jnp.dot(jnp.concatenate([high, low], axis=1), ww[...], preferred_element_type=F32)

        def member(mm, total):
            fine = fbuf[rows_at(mm * 8, 8), :]
            return tuple(total[l] + fine * pert[first + mm, l].astype(F32) for l in range(LEVELS))

        total = lax.fori_loop(0, GROUP, member, tuple(ens[l] for l in range(LEVELS)), unroll=2)
        for l in range(LEVELS):
            ens[l] = total[l]
        return _

    lax.fori_loop(0, BEFORE, ensemble_group, 0)

    for copy in lev_copies[:2] + static_rows:
        copy.wait_recv()
    to_rows(nat_s, v_s, lambda value: value)
    to_rows(nat_k, kap, jnp.sqrt)
    unpack_rows(from_rows, 0, v_s, lambda value: value)
    unpack_rows(from_rows, PACKED, kap, jnp.sqrt)
    loads[9].wait()
    kap[0:HALO] = jnp.where(w == 0, 0.0, kap[0:HALO])
    kap[11 * 64 : ALL_ROWS] = jnp.where(w == WIDE - 1, 0.0, kap[11 * 64 : ALL_ROWS])
    diffuse(v_s)
    to_natural(v_s, tmp)
    lax.fori_loop(BEFORE, 8, ensemble_group, 0)

    for i in (6, 7, 8):
        loads[i].wait()
    j = lax.broadcasted_iota(jnp.int32, (WIDE, 1024), 0)
    x = lax.broadcasted_iota(jnp.int32, (WIDE, 1024), 1)
    spread = jnp.where(x // 8 == j, 1.0, 0.0).astype(BF16)
    blocks = jnp.concatenate([jnp.where(hub[0:LEVELS] == 1, 1.0, 0.0), jnp.zeros((12, 128), F32)], axis=0).astype(BF16)
    hubx[...] = jnp.dot(blocks, spread, preferred_element_type=F32)
    for t in range(TILES):
        columns = slice(t * 128, t * 128 + 128)
        ocean = mask[t * 8 : t * 8 + 8].astype(F32)
        for l in range(LEVELS):
            at = (l * TILES + t) * 8
            there = rows_at(own0 + at, 8)
            inc = ocean * (SCALE * ens[l, :, columns] + tmp[there, :])
            incb[at : at + 8] = inc
            misfit = inc - inn[at : at + 8]
            is_huber = jnp.broadcast_to(hubx[l : l + 1, columns], (8, 128)) > 0.5
            weight = jnp.where(is_huber, 1.0 / jnp.maximum(jnp.abs(misfit), 1.0), 1.0)
            weighted = ocean * weight * misfit
            nat_w[there, :] = weighted
            wsc[l, :, columns] = weighted * SCALE
    lev_copies[2].start()
    pack_rows(nat_w, pack_w, 0)
    for copy in weighted_rows:
        copy.start()
    inc_out = pltpu.make_async_copy(incb, inc_hbm, out_sem.at[0])
    inc_out.start()

    def adjoint_group(i, first_place):
        first = ((group + i) % GROUPS) * GROUP

        def member(mm, _):
            total = pert[first + mm, 0].astype(F32) * wsc[0]
            for l in range(1, LEVELS):
                total = total + pert[first + mm, l].astype(F32) * wsc[l]
            fbuf[rows_at(mm * 8, 8), :] = total
            return _

        lax.fori_loop(0, GROUP, member, 0, unroll=2)
        high = fbuf[...].astype(BF16)
        low = (fbuf[...] - high.astype(F32)).astype(BF16)
        gbuf[...] = jnp.dot(high, wt[...], preferred_element_type=F32) + jnp.dot(
            low, wt[...], preferred_element_type=F32
        )
        below = gbuf[pl.ds(0, GROUP, stride=8), :]
        above = jnp.zeros((GROUP, 128), F32)
        for r in range(1, 8):
            row = gbuf[pl.ds(r, GROUP, stride=8), :]
            below = below + row * (1.0 - r * 0.125)
            above = above + row * (r * 0.125)
        sb[pl.ds(2 * first, GROUP, stride=2), :] = below
        sb[pl.ds(2 * first + 1, GROUP, stride=2), :] = above

        def send(n, _):
            member_at = first + (place + n) % GROUP
            remote(
                sb.at[pl.ds(2 * member_at, 2)], bb.at[pl.ds(2 * w, 2)], bwd_send, bwd_recv, wide=member_at
            ).start()
            return _

        lax.fori_loop(first_place, GROUP, send, 0)

    def adjoint_far(n, _):
        adjoint_group(offset_of(n), 0)
        return _

    lax.fori_loop(0, 7, adjoint_far, 0)
    adjoint_group(0, 1)
    mine = pl.ds(2 * w, 2)
    pltpu.make_async_copy(sb.at[mine], bb.at[mine], bwd_recv).start()

    def weighted_diffusion():
        for copy in [lev_copies[2]] + weighted_rows:
            copy.wait_recv()
        to_rows(nat_w, v_w, lambda value: value)
        unpack_rows(from_rows_w, 0, v_w, lambda value: value)
        diffuse(v_w)
        to_natural(v_w, tmp)
        sgb[...] = nat_s[pl.ds(own0, OWN), :] + tmp[pl.ds(own0, OWN), :]

    def half_gradient():
        wait_bytes(bb, bwd_recv)
        half[...] = lax.dot_general(
            r2[...], bb[...], (((0,), (0,)), ((), ())), precision=PRECISE, preferred_element_type=F32
        )
        half_copy.start()

    half_copy = remote(half, twin, half_send, half_recv, level=1 - lev)
    if D_FIRST:
        weighted_diffusion()
        half_gradient()
    else:
        half_gradient()
        weighted_diffusion()
    sg_out = pltpu.make_async_copy(sgb, sg_hbm, out_sem.at[1])
    sg_out.start()

    half_copy.wait_recv()
    mgb[...] = mc[...] + lax.dot_general(
        half[...] + twin[...], cf[...], (((1,), (1,)), ((), ())), precision=PRECISE, preferred_element_type=F32
    )
    mg_out = pltpu.make_async_copy(mgb, mg_hbm, out_sem.at[2])
    mg_out.start()

    wait_bytes(ext.at[pl.ds(0, 254)], fwd_send)
    wait_bytes(ext.at[pl.ds(0, 254)], bwd_send)
    for copy in lev_copies + static_rows + weighted_rows + [half_copy]:
        copy.wait_send()
    inc_out.wait()
    sg_out.wait()
    mg_out.wait()


def finish(*refs):
    sources, results, held, sem = refs[:3], refs[3:6], refs[6:9], refs[9]
    inward = [pltpu.make_async_copy(a, b, sem.at[0, i]) for i, (a, b) in enumerate(zip(sources, held))]
    outward = [pltpu.make_async_copy(a, b, sem.at[1, i]) for i, (a, b) in enumerate(zip(held, results))]
    for copy in inward:
        copy.start()
    for into, out in zip(inward, outward):
        into.wait()
        out.start()
    for copy in outward:
        copy.wait()


def natural(array):
    levels = array.shape[0]
    return array.reshape(levels, 8, TILES, 128).transpose(0, 2, 1, 3).reshape(levels * 64, 128)


def from_natural(array):
    return array.reshape(LEVELS, TILES, 8, 128).transpose(0, 2, 1, 3).reshape(LEVELS, 8, 1024)


def on_device(
    member_control, static_control, perturbations, innovation, diffusivity,
    rows_factor, column_factor, ocean_mask, huber_blocks, fold_map,
):
    hbm = pl.BlockSpec(memory_space=pltpu.HBM)
    dma = pltpu.SemaphoreType.DMA

    def vmem(*shape, dtype=F32):
        return pltpu.VMEM(shape, dtype)

    increment, member_gradient, static_gradient = pl.pallas_call(
        kernel,
        out_shape=(
            jax.ShapeDtypeStruct((OWN, 128), F32),
            jax.ShapeDtypeStruct((128, 128), F32),
            jax.ShapeDtypeStruct((OWN, 128), F32),
        ),
        in_specs=[hbm] * 10,
        out_specs=[hbm] * 3,
        scratch_shapes=[
            vmem(WIDE, LEVELS, 8, 1024, dtype=BF16),
            vmem(128, 128), vmem(128, 128), vmem(256, 128),
            vmem(256, 128), vmem(256, 128), vmem(256, 128), vmem(256, 128),
            vmem(512, 128), vmem(512, 128), vmem(512, 128),
            vmem(OWN, 128), vmem(64, 128, dtype=jnp.int32), vmem(8, 128, dtype=jnp.int32),
            vmem(8, 128, dtype=jnp.int32),
            vmem(ALL_ROWS, 128), vmem(ALL_ROWS, 128), vmem(ALL_ROWS, 128),
            vmem(ALL_ROWS, 128), vmem(ALL_ROWS, 128),
            vmem(512, 128),
            vmem(256, 1024, dtype=BF16), vmem(1024, 128, dtype=BF16),
            vmem(128, 128), vmem(128, 1024), vmem(128, 128),
            vmem(LEVELS, 8, 1024), vmem(LEVELS, 8, 1024), vmem(16, 1024),
            vmem(OWN, 128), vmem(OWN, 128), vmem(128, 128),
            vmem(2 * PACKED, 128), vmem(PACKED, 128), vmem(2 * PACKED, 128), vmem(PACKED, 128),
            vmem(128, 128), vmem(128, 128), vmem(WIDE, 1024),
            dma((10,)), dma((3,)), dma, dma((8,)), dma, dma, dma((3,)), dma((3,)), dma((12,)), dma((12,)), dma, dma,
        ],
        compiler_params=pltpu.CompilerParams(
            collective_id=0, has_side_effects=True, vmem_limit_bytes=63 << 20
        ),
        name="increment_and_gradients",
    )(
        member_control.reshape(128, 128),
        natural(static_control),
        perturbations,
        natural(innovation),
        natural(diffusivity),
        rows_factor,
        column_factor,
        natural(ocean_mask[None]),
        huber_blocks.reshape(LEVELS, 128),
        fold_map.reshape(8, 128),
    )
    increment, member_gradient, static_gradient = pl.pallas_call(
        finish,
        out_shape=(
            jax.ShapeDtypeStruct((OWN, 128), F32),
            jax.ShapeDtypeStruct((128, 128), F32),
            jax.ShapeDtypeStruct((OWN, 128), F32),
        ),
        in_specs=[hbm] * 3,
        out_specs=[hbm] * 3,
        scratch_shapes=[vmem(OWN, 128), vmem(128, 128), vmem(OWN, 128), dma((2, 3))],
        compiler_params=pltpu.CompilerParams(vmem_limit_bytes=63 << 20),
        name="finish",
    )(increment, member_gradient, static_gradient)
    return from_natural(increment), member_gradient[None], from_natural(static_gradient)


def solution(mesh):
    return jax.shard_map(
        on_device,
        mesh=mesh,
        in_specs=(
            P("wide", None, None),
            P("lev", "wide", None),
            P(None, "lev", "wide", None),
            P("lev", "wide", None),
            P("lev", "wide", None),
            P(),
            P(),
            P("wide", None),
            P("lev", "wide", None),
            P(),
        ),
        out_specs=(P("lev", "wide", None), P("wide", None, None), P("lev", "wide", None)),
        check_vma=False,
    )
```

```python
import functools

import jax
import jax.numpy as jnp
from jax import lax
from jax.experimental import pallas as pl
from jax.experimental.pallas import tpu as pltpu
from jax.sharding import PartitionSpec as P

STEPS = 3
WIDE = 128
GROUP = 16
GROUPS = WIDE // GROUP
D_FIRST = False
BEFORE = 3
LEVELS = 4
TILES = 8
F32 = jnp.float32
BF16 = jnp.bfloat16
MESH = pl.DeviceIdType.MESH
PRECISE = lax.Precision.HIGHEST
SCALE = 127.0 ** (-0.5)
OWN = LEVELS * 64
HALO = STEPS * 64
ALL_ROWS = (8 + 2 * STEPS) * 64
DOWN_SIZE = STEPS * LEVELS * 8
PACKED = 2 * DOWN_SIZE + 48


def rows_at(start, size, step=1):
    if step == 1:
        return pl.ds(pl.multiple_of(start, 8), size)
    return pl.ds(start, size, stride=step)


def kernel(
    mc_hbm, sc_hbm, pert_hbm, inn_hbm, dif_hbm, rf_hbm, cf_hbm, mask_hbm, hub_hbm, fold_hbm,
    inc_hbm, mg_hbm, sg_hbm,
    pert, mc, cf, r2, win, ext, bb, sb, nat_s, nat_k, nat_w, inn, mask, hub, fold,
    v_s, v_w, kap, s_a, s_b, tmp, ww, wt, parts, fbuf, gbuf, ens, wsc, hubx, incb, sgb, mgb,
    pack, pack_w, from_rows, from_rows_w, half, twin, table, bb_late,
    load_sem, out_sem, fwd_send, fwd_recv, bwd_send, bwd_recv, lev_send, lev_recv, row_send, row_recv, half_send, half_recv,
):
    w = lax.axis_index("wide")
    lev = lax.axis_index("lev")
    group, place = w // GROUP, w % GROUP
    right, left = (w + 1) % WIDE, (w + WIDE - 1) % WIDE
    own0 = pl.multiple_of(lev * OWN, OWN)

    def remote(src, dst, send, recv, wide=None, level=None):
        target = {"wide": w if wide is None else wide, "lev": lev if level is None else level}
        return pltpu.make_async_remote_copy(
            src_ref=src, dst_ref=dst, send_sem=send, recv_sem=recv, device_id=target, device_id_type=MESH
        )

    def wait_bytes(ref, sem):
        pltpu.make_async_copy(ref, ref, sem).wait()

    loads = [
        (mc_hbm, mc), (cf_hbm, cf), (rf_hbm, tmp.at[pl.ds(0, 128)]),
        (sc_hbm, nat_s.at[pl.ds(own0, OWN)]), (dif_hbm, nat_k.at[pl.ds(own0, OWN)]),
        (pert_hbm, pert), (inn_hbm, inn), (mask_hbm, mask), (hub_hbm, hub.at[pl.ds(0, LEVELS)]), (fold_hbm, fold),
    ]
    loads = [pltpu.make_async_copy(src, dst, load_sem.at[i]) for i, (src, dst) in enumerate(loads)]
    for load in loads:
        load.start()

    barrier = pltpu.get_barrier_semaphore()

    def signal(wide, level):
        pl.semaphore_signal(barrier, inc=1, device_id={"wide": wide, "lev": level}, device_id_type=MESH)

    for wide in (w, left, right):
        signal(wide, 1 - lev)

    column = lax.broadcasted_iota(jnp.int32, (8, 1024), 1)
    cell, part = column // 8, (column % 8).astype(F32) * 0.125

    def table_and_signals(n, _):
        j = lax.broadcasted_iota(jnp.int32, (8, 1024), 0) + n * 8
        both = jnp.where(cell == j, 1.0 - part, 0.0) + jnp.where((cell + 1) % WIDE == j, part, 0.0)
        table[rows_at(n * 8, 8), :] = both
        for k in range(8):
            signal((w + n * 8 + k + 1) % WIDE, lev)
        return _

    lax.fori_loop(0, 15, table_and_signals, 0)
    j = lax.broadcasted_iota(jnp.int32, (8, 1024), 0) + 120
    table[120:128] = jnp.where(cell == j, 1.0 - part, 0.0) + jnp.where((cell + 1) % WIDE == j, part, 0.0)
    for k in range(7):
        signal((w + 121 + k) % WIDE, lev)
    weights = table[...].astype(BF16)
    ww[0:128] = weights
    ww[128:256] = weights
    wt[...] = table[...].T.astype(BF16)

    for i in range(3):
        loads[i].wait()
    r2[pl.ds(0, 128, stride=2), :] = tmp[0:128]
    r2[pl.ds(1, 128, stride=2), :] = jnp.concatenate([tmp[1:128], tmp[127:128]], axis=0)
    columns_done = jnp.dot(mc[...], cf[...], precision=PRECISE, preferred_element_type=F32)
    win[...] = jnp.dot(r2[...], columns_done, precision=PRECISE, preferred_element_type=F32)

    near, next_near = 3 * (1 - lev), 2 - lev

    def pack_rows(nat, out, at):
        def row(level, r):
            return nat[pl.ds(own0 + level * 64 + r, 8, stride=8), :]

        for k in range(STEPS):
            for l in range(LEVELS):
                out[pl.ds(at + (k * LEVELS + l) * 8, 8), :] = row(l, 5 + k)
                out[pl.ds(at + DOWN_SIZE + (k * LEVELS + l) * 8, 8), :] = row(l, k)
        for k, (level, r) in enumerate(((near, 7), (near, 6), (next_near, 7), (near, 0), (near, 1), (next_near, 0))):
            out[pl.ds(at + 2 * DOWN_SIZE + k * 8, 8), :] = row(level, r)

    def unpack_rows(got, at, out, change):
        def put(r, level, value):
            out[pl.ds(r * 64 + level, 8, stride=8), :] = change(value)

        for k in range(STEPS):
            for l in range(LEVELS):
                put(k, lev * LEVELS + l, got[pl.ds(at + (k * LEVELS + l) * 8, 8), :])
                put(11 + k, lev * LEVELS + l, got[pl.ds(at + DOWN_SIZE + (k * LEVELS + l) * 8, 8), :])
        theirs, theirs_next = 4 - lev, 5 - 3 * lev
        for k, (r, level) in enumerate(
            ((2, theirs), (1, theirs), (2, theirs_next), (11, theirs), (12, theirs), (11, theirs_next))
        ):
            put(r, level, got[pl.ds(at + 2 * DOWN_SIZE + k * 8, 8), :])

    def row_copies(out, got, at, i):
        parts = (
            (right, lev, 0, DOWN_SIZE), (left, lev, DOWN_SIZE, DOWN_SIZE),
            (right, 1 - lev, 2 * DOWN_SIZE, 24), (left, 1 - lev, 2 * DOWN_SIZE + 24, 24),
        )
        return [
            remote(
                out.at[pl.ds(at + start, size)], got.at[pl.ds(at + start, size)],
                row_send.at[i + k], row_recv.at[i + k], wide=wide, level=level,
            )
            for k, (wide, level, start, size) in enumerate(parts)
        ]

    seen = pl.ds(pl.multiple_of(64 + 192 * lev, 64), 192)
    unseen = pl.ds(pl.multiple_of(448 * (1 - lev), 64), 64)
    lev_copies = [
        remote(nat.at[seen], nat.at[seen], lev_send.at[i], lev_recv.at[i], level=1 - lev)
        for i, nat in enumerate((nat_s, nat_k, nat_w))
    ]
    static_rows = row_copies(pack, from_rows, 0, 0) + row_copies(pack, from_rows, PACKED, 4)
    weighted_rows = row_copies(pack_w, from_rows_w, 0, 8)
    for i in (3, 4):
        loads[i].wait()
    pack_rows(nat_s, pack, 0)
    pack_rows(nat_k, pack, PACKED)
    for nat in (nat_s, nat_k, nat_w):
        nat[unseen, :] = jnp.zeros((64, 128), F32)
    for rows in (v_s, v_w, kap):
        rows[0:HALO] = jnp.zeros((HALO, 128), F32)
        rows[11 * 64 : ALL_ROWS] = jnp.zeros((HALO, 128), F32)

    pl.semaphore_wait(barrier, WIDE + 2)
    lev_copies[0].start()
    lev_copies[1].start()
    for copy in static_rows:
        copy.start()

    def near_first(n):
        return n + (n // 2) * (5 - 2 * n)

    def send_window(n, _):
        i = near_first(n // (2 * GROUP)) + 4 * (n // GROUP % 2)
        to = ((group + i) % GROUPS) * GROUP + (place + n % GROUP) % GROUP
        remote(win.at[pl.ds(2 * to, 2)], ext.at[pl.ds(2 * w, 2)], fwd_send, fwd_recv.at[i], wide=to).start()
        return _

    lax.fori_loop(1, WIDE, send_window, 0)
    pltpu.make_async_copy(win.at[pl.ds(2 * w, 2)], ext.at[pl.ds(2 * w, 2)], fwd_recv.at[0]).start()

    def to_rows(nat, out, change):
        def body(r, _):
            for t in range(TILES):
                out[rows_at((r + STEPS) * 64 + t * 8, 8), :] = change(nat[rows_at(t * 8 + r, 8, 64), :])
            return _

        lax.fori_loop(0, 8, body, 0)

    def to_natural(rows, out):
        def body(r, _):
            for t in range(TILES):
                out[rows_at(t * 8 + r, 8, 64), :] = rows[rows_at((r + STEPS) * 64 + t * 8, 8), :]
            return _

        lax.fori_loop(0, 8, body, 0)

    sublane = lax.broadcasted_iota(jnp.int32, (8, 8, 128), 1)
    lane = lax.broadcasted_iota(jnp.int32, (64, 128), 1)

    def fold_row(s_buf):
        def body(t, _):
            entry = jnp.broadcast_to(fold[pl.ds(t, 1), :], (8, 128))
            at, tile = entry % 128, entry // 128
            total = jnp.zeros((8, 128), F32)
            for u in range(TILES):
                there = jnp.take_along_axis(
                    s_buf[pl.ds(10 * 64 + u * 8, 8), :], at, axis=1, mode="promise_in_bounds"
                )
                total = jnp.where(tile == u, there, total)
            s_buf[rows_at(11 * 64 + t * 8, 8), :] = total
            return _

        @pl.when(w == WIDE - 1)
        def _():
            lax.fori_loop(0, TILES, body, 0, unroll=4)

    def diffuse(v):
        def scale_row(i, _):
            here = rows_at(i * 64, 64)
            s_a[here, :] = kap[here, :] * v[here, :]
            return _

        lax.fori_loop(0, 14, scale_row, 0, unroll=2)
        for step in range(1, STEPS + 1):
            s_buf, s_next = (s_a, s_b) if step % 2 else (s_b, s_a)
            fold_row(s_buf)

            def update_row(i, _):
                here = rows_at(i * 64, 64)
                s = s_buf[here, :]
                after = pltpu.roll(s, 1, 1)
                before = pltpu.roll(s, 127, 1)
                west = jnp.where(lane == 0, jnp.concatenate([after[56:], after[:56]], axis=0), after)
                east = jnp.where(lane == 127, jnp.concatenate([before[8:], before[:8]], axis=0), before)
                s3 = s.reshape(8, 8, 128)
                below = jnp.where(sublane == 0, 0.0, pltpu.roll(s3, 1, 1)).reshape(64, 128)
                above = jnp.where(sublane == 7, 0.0, pltpu.roll(s3, 7, 1)).reshape(64, 128)
                across = s_buf[rows_at(i * 64 + 64, 64), :] + s_buf[rows_at(i * 64 - 64, 64), :] + west + east
                new = v[here, :] + kap[here, :] * (across + 0.5 * (below + above) - 5.0 * s)
                v[here, :] = new
                if step < STEPS:
                    s_next[here, :] = kap[here, :] * new
                return _

            lax.fori_loop(step, 14 - step, update_row, 0, unroll=4)

    eighth = lax.broadcasted_iota(jnp.int32, (8, 1024), 0).astype(F32) * 0.125
    loads[5].wait()
    ens[...] = jnp.zeros((LEVELS, 8, 1024), F32)

    def ensemble_pair(n, _):
        firsts = []
        for i in (near_first(n), near_first(n) + 4):
            wait_bytes(ext.at[pl.ds(0, 2 * GROUP)], fwd_recv.at[i])
            firsts.append(((group + GROUPS - i) % GROUPS) * GROUP)
        coarse = jnp.concatenate([ext[rows_at(2 * first, 2 * GROUP), :] for first in firsts], axis=0)
        high = coarse.astype(BF16)
        low = (coarse - high.astype(F32)).astype(BF16)
        fbuf[0 : 4 * GROUP] = jnp.dot(
            jnp.concatenate([high, low], axis=1), ww[...], preferred_element_type=F32
        )
        total = tuple(ens[l] for l in range(LEVELS))
        for k, first in enumerate(firsts):

            def member(mm, total):
                at = 2 * GROUP * k + 2 * mm
                row = jnp.broadcast_to(fbuf[pl.ds(at, 1), :], (8, 1024))
                after = jnp.broadcast_to(fbuf[pl.ds(at + 1, 1), :], (8, 1024))
                fine = row + (after - row) * eighth
                return tuple(total[l] + fine * pert[first + mm, l].astype(F32) for l in range(LEVELS))

            total = lax.fori_loop(0, GROUP, member, total, unroll=2)
        for l in range(LEVELS):
            ens[l] = total[l]
        return _

    lax.fori_loop(0, BEFORE, ensemble_pair, 0)

    for copy in lev_copies[:2] + static_rows:
        copy.wait_recv()
    to_rows(nat_s, v_s, lambda value: value)
    to_rows(nat_k, kap, jnp.sqrt)
    unpack_rows(from_rows, 0, v_s, lambda value: value)
    unpack_rows(from_rows, PACKED, kap, jnp.sqrt)
    loads[9].wait()
    kap[0:HALO] = jnp.where(w == 0, 0.0, kap[0:HALO])
    kap[11 * 64 : ALL_ROWS] = jnp.where(w == WIDE - 1, 0.0, kap[11 * 64 : ALL_ROWS])
    diffuse(v_s)
    to_natural(v_s, tmp)
    lax.fori_loop(BEFORE, 4, ensemble_pair, 0)

    for i in (6, 7, 8):
        loads[i].wait()
    j = lax.broadcasted_iota(jnp.int32, (WIDE, 1024), 0)
    x = lax.broadcasted_iota(jnp.int32, (WIDE, 1024), 1)
    spread = jnp.where(x // 8 == j, 1.0, 0.0).astype(BF16)
    blocks = jnp.concatenate([jnp.where(hub[0:LEVELS] == 1, 1.0, 0.0), jnp.zeros((12, 128), F32)], axis=0).astype(BF16)
    hubx[...] = jnp.dot(blocks, spread, preferred_element_type=F32)
    for t in range(TILES):
        columns = slice(t * 128, t * 128 + 128)
        ocean = mask[t * 8 : t * 8 + 8].astype(F32)
        for l in range(LEVELS):
            at = (l * TILES + t) * 8
            there = rows_at(own0 + at, 8)
            inc = ocean * (SCALE * ens[l, :, columns] + tmp[there, :])
            incb[at : at + 8] = inc
            misfit = inc - inn[at : at + 8]
            is_huber = jnp.broadcast_to(hubx[l : l + 1, columns], (8, 128)) > 0.5
            weight = jnp.where(is_huber, 1.0 / jnp.maximum(jnp.abs(misfit), 1.0), 1.0)
            weighted = ocean * weight * misfit
            nat_w[there, :] = weighted
            wsc[l, :, columns] = weighted * SCALE
    lev_copies[2].start()
    pack_rows(nat_w, pack_w, 0)
    for copy in weighted_rows:
        copy.start()
    inc_out = pltpu.make_async_copy(incb, inc_hbm, out_sem.at[0])
    inc_out.start()

    def adjoint_pair(n, offsets, late):
        firsts = [((group + i) % GROUPS) * GROUP for i in offsets]
        for k, first in enumerate(firsts):

            def member(mm, _):
                total = pert[first + mm, 0].astype(F32) * wsc[0]
                for l in range(1, LEVELS):
                    total = total + pert[first + mm, l].astype(F32) * wsc[l]
                fbuf[rows_at((GROUP * k + mm) * 8, 8), :] = total
                return _

            lax.fori_loop(0, GROUP, member, 0, unroll=2)
        terms = fbuf[...]
        high = terms.astype(BF16)
        parts[0:256] = high
        parts[256:512] = (terms - high.astype(F32)).astype(BF16)
        columns_done = jnp.dot(parts[...], wt[...], preferred_element_type=F32)
        gbuf[...] = columns_done[0:256] + columns_done[256:512]
        below = gbuf[pl.ds(0, 2 * GROUP, stride=8), :]
        above = jnp.zeros((2 * GROUP, 128), F32)
        for r in range(1, 8):
            row = gbuf[pl.ds(r, 2 * GROUP, stride=8), :]
            below = below + row * (1.0 - r * 0.125)
            above = above + row * (r * 0.125)
        for k, first in enumerate(firsts):
            sb[pl.ds(2 * first, GROUP, stride=2), :] = below[k * GROUP : (k + 1) * GROUP]
            sb[pl.ds(2 * first + 1, GROUP, stride=2), :] = above[k * GROUP : (k + 1) * GROUP]

            def send(p, _):
                member_at = first + (place + p) % GROUP
                source = sb.at[pl.ds(2 * member_at, 2)]
                if late:
                    slot = bb_late.at[pl.ds(2 * (64 * lev + (2 * n - 4 + k) * GROUP + place), 2)]
                    remote(source, slot, bwd_send, bwd_recv.at[1], wide=member_at, level=1 - lev).start()
                else:
                    slot = bb.at[pl.ds(2 * ((2 * n + k) * GROUP + place), 2)]
                remote(source, slot, bwd_send, bwd_recv.at[1 if late else 0], wide=member_at).start()
                return _

            lax.fori_loop(1 if late and offsets[k] == 0 else 0, GROUP, send, 0)

    def adjoint_far(n, _):
        adjoint_pair(n, (2 - n, 6 - n), False)
        return _

    lax.fori_loop(0, 2, adjoint_far, 0)
    adjoint_pair(2, (3, 7), True)
    adjoint_pair(3, (4, 0), True)
    mine = pl.ds(2 * w, 2)
    slot = pl.ds(2 * (64 * lev + 3 * GROUP + place), 2)
    remote(sb.at[mine], bb_late.at[slot], bwd_send, bwd_recv.at[1], level=1 - lev).start()
    pltpu.make_async_copy(sb.at[mine], bb_late.at[slot], bwd_recv.at[1]).start()

    def weighted_diffusion():
        for copy in [lev_copies[2]] + weighted_rows:
            copy.wait_recv()
        to_rows(nat_w, v_w, lambda value: value)
        unpack_rows(from_rows_w, 0, v_w, lambda value: value)
        diffuse(v_w)
        to_natural(v_w, tmp)
        sgb[...] = nat_s[pl.ds(own0, OWN), :] + tmp[pl.ds(own0, OWN), :]

    def rows_adjoint(terms, offsets):
        blocks = [r2[rows_at(((group + GROUPS - i) % GROUPS) * 2 * GROUP, 2 * GROUP), :] for i in offsets]
        return lax.dot_general(
            jnp.concatenate(blocks, axis=0), terms, (((0,), (0,)), ((), ())),
            precision=PRECISE, preferred_element_type=F32,
        )

    def half_gradient():
        wait_bytes(bb, bwd_recv.at[0])
        half[...] = rows_adjoint(bb[...], (2, 6, 1, 5))
        half_copy.start()

    half_copy = remote(half, twin, half_send, half_recv, level=1 - lev)
    if D_FIRST:
        weighted_diffusion()
        half_gradient()
    else:
        half_gradient()
        weighted_diffusion()
    sg_out = pltpu.make_async_copy(sgb, sg_hbm, out_sem.at[1])
    sg_out.start()

    wait_bytes(bb_late, bwd_recv.at[1])
    rows_done = half[...] + rows_adjoint(bb_late[0:128] + bb_late[128:256], (3, 7, 4, 0))
    half_copy.wait_recv()
    mgb[...] = mc[...] + lax.dot_general(
        rows_done + twin[...], cf[...], (((1,), (1,)), ((), ())), precision=PRECISE, preferred_element_type=F32
    )
    mg_out = pltpu.make_async_copy(mgb, mg_hbm, out_sem.at[2])
    mg_out.start()

    wait_bytes(ext.at[pl.ds(0, 254)], fwd_send)
    wait_bytes(nat_s.at[pl.ds(0, 2 * 192 - 2)], bwd_send)
    for copy in lev_copies + static_rows + weighted_rows + [half_copy]:
        copy.wait_send()
    inc_out.wait()
    sg_out.wait()
    mg_out.wait()


def finish(*refs):
    sources, results, held, sem = refs[:3], refs[3:6], refs[6:9], refs[9]
    inward = [pltpu.make_async_copy(a, b, sem.at[0, i]) for i, (a, b) in enumerate(zip(sources, held))]
    outward = [pltpu.make_async_copy(a, b, sem.at[1, i]) for i, (a, b) in enumerate(zip(held, results))]
    for copy in inward:
        copy.start()
    for into, out in zip(inward, outward):
        into.wait()
        out.start()
    for copy in outward:
        copy.wait()


def natural(array):
    levels = array.shape[0]
    return array.reshape(levels, 8, TILES, 128).transpose(0, 2, 1, 3).reshape(levels * 64, 128)


def from_natural(array):
    return array.reshape(LEVELS, TILES, 8, 128).transpose(0, 2, 1, 3).reshape(LEVELS, 8, 1024)


def on_device(
    member_control, static_control, perturbations, innovation, diffusivity,
    rows_factor, column_factor, ocean_mask, huber_blocks, fold_map,
):
    hbm = pl.BlockSpec(memory_space=pltpu.HBM)
    dma = pltpu.SemaphoreType.DMA

    def vmem(*shape, dtype=F32):
        return pltpu.VMEM(shape, dtype)

    increment, member_gradient, static_gradient = pl.pallas_call(
        kernel,
        out_shape=(
            jax.ShapeDtypeStruct((OWN, 128), F32),
            jax.ShapeDtypeStruct((128, 128), F32),
            jax.ShapeDtypeStruct((OWN, 128), F32),
        ),
        in_specs=[hbm] * 10,
        out_specs=[hbm] * 3,
        scratch_shapes=[
            vmem(WIDE, LEVELS, 8, 1024, dtype=BF16),
            vmem(128, 128), vmem(128, 128), vmem(256, 128),
            vmem(256, 128), vmem(256, 128), vmem(128, 128), vmem(256, 128),
            vmem(512, 128), vmem(512, 128), vmem(512, 128),
            vmem(OWN, 128), vmem(64, 128, dtype=jnp.int32), vmem(8, 128, dtype=jnp.int32),
            vmem(8, 128, dtype=jnp.int32),
            vmem(ALL_ROWS, 128), vmem(ALL_ROWS, 128), vmem(ALL_ROWS, 128),
            vmem(ALL_ROWS, 128), vmem(ALL_ROWS, 128),
            vmem(512, 128),
            vmem(256, 1024, dtype=BF16), vmem(1024, 128, dtype=BF16),
            vmem(512, 1024, dtype=BF16), vmem(256, 1024), vmem(256, 128),
            vmem(LEVELS, 8, 1024), vmem(LEVELS, 8, 1024), vmem(16, 1024),
            vmem(OWN, 128), vmem(OWN, 128), vmem(128, 128),
            vmem(2 * PACKED, 128), vmem(PACKED, 128), vmem(2 * PACKED, 128), vmem(PACKED, 128),
            vmem(128, 128), vmem(128, 128), vmem(WIDE, 1024), vmem(256, 128),
            dma((10,)), dma((3,)), dma, dma((8,)), dma, dma((2,)), dma((3,)), dma((3,)), dma((12,)), dma((12,)), dma, dma,
        ],
        compiler_params=pltpu.CompilerParams(
            collective_id=0, has_side_effects=True, vmem_limit_bytes=63 << 20
        ),
        name="increment_and_gradients",
    )(
        member_control.reshape(128, 128),
        natural(static_control),
        perturbations,
        natural(innovation),
        natural(diffusivity),
        rows_factor,
        column_factor,
        natural(ocean_mask[None]),
        huber_blocks.reshape(LEVELS, 128),
        fold_map.reshape(8, 128),
    )
    increment, member_gradient, static_gradient = pl.pallas_call(
        finish,
        out_shape=(
            jax.ShapeDtypeStruct((OWN, 128), F32),
            jax.ShapeDtypeStruct((128, 128), F32),
            jax.ShapeDtypeStruct((OWN, 128), F32),
        ),
        in_specs=[hbm] * 3,
        out_specs=[hbm] * 3,
        scratch_shapes=[vmem(OWN, 128), vmem(128, 128), vmem(OWN, 128), dma((2, 3))],
        compiler_params=pltpu.CompilerParams(vmem_limit_bytes=63 << 20),
        name="finish",
    )(increment, member_gradient, static_gradient)
    return from_natural(increment), member_gradient[None], from_natural(static_gradient)


def solution(mesh):
    return jax.shard_map(
        on_device,
        mesh=mesh,
        in_specs=(
            P("wide", None, None),
            P("lev", "wide", None),
            P(None, "lev", "wide", None),
            P("lev", "wide", None),
            P("lev", "wide", None),
            P(),
            P(),
            P("wide", None),
            P("lev", "wide", None),
            P(),
        ),
        out_specs=(P("lev", "wide", None), P("wide", None, None), P("lev", "wide", None)),
        check_vma=False,
    )
```

```python
import functools

import jax
import jax.numpy as jnp
from jax import lax
from jax.experimental import pallas as pl
from jax.experimental.pallas import tpu as pltpu
from jax.sharding import PartitionSpec as P

STEPS = 3
WIDE = 128
GROUP = 16
GROUPS = WIDE // GROUP
D_FIRST = False
EARLY = 2
PAIRS = ((2, 6), (1, 7), (3, 5), (4, 0))
LATE_TILES = (4 - EARLY) * 2 * GROUP
BEFORE = 3
LEVELS = 4
TILES = 8
F32 = jnp.float32
BF16 = jnp.bfloat16
MESH = pl.DeviceIdType.MESH
PRECISE = lax.Precision.HIGHEST
SCALE = 127.0 ** (-0.5)
OWN = LEVELS * 64
HALO = STEPS * 64
ALL_ROWS = (8 + 2 * STEPS) * 64
DOWN_SIZE = STEPS * LEVELS * 8
PACKED = 2 * DOWN_SIZE + 48


def rows_at(start, size, step=1):
    if step == 1:
        return pl.ds(pl.multiple_of(start, 8), size)
    return pl.ds(start, size, stride=step)


def kernel(
    mc_hbm, sc_hbm, pert_hbm, inn_hbm, dif_hbm, rf_hbm, cf_hbm, mask_hbm, hub_hbm, fold_hbm,
    inc_hbm, mg_hbm, sg_hbm,
    pert, mc, cf, r2, win, ext, bb, sb, nat_s, nat_k, nat_w, inn, mask, hub, fold,
    v_s, v_w, kap, s_a, s_b, tmp, ww, wt, parts, fbuf, gbuf, ens, wsc, hubx, incb, sgb, mgb,
    pack, pack_w, from_rows, from_rows_w, half, twin, table, bb_late,
    load_sem, out_sem, fwd_send, fwd_recv, bwd_send, bwd_recv, lev_send, lev_recv, row_send, row_recv, half_send, half_recv,
):
    w = lax.axis_index("wide")
    lev = lax.axis_index("lev")
    group, place = w // GROUP, w % GROUP
    right, left = (w + 1) % WIDE, (w + WIDE - 1) % WIDE
    own0 = pl.multiple_of(lev * OWN, OWN)

    def remote(src, dst, send, recv, wide=None, level=None):
        target = {"wide": w if wide is None else wide, "lev": lev if level is None else level}
        return pltpu.make_async_remote_copy(
            src_ref=src, dst_ref=dst, send_sem=send, recv_sem=recv, device_id=target, device_id_type=MESH
        )

    def wait_bytes(ref, sem):
        pltpu.make_async_copy(ref, ref, sem).wait()

    loads = [
        (mc_hbm, mc), (cf_hbm, cf), (rf_hbm, tmp.at[pl.ds(0, 128)]),
        (sc_hbm, nat_s.at[pl.ds(own0, OWN)]), (dif_hbm, nat_k.at[pl.ds(own0, OWN)]),
        (pert_hbm, pert), (inn_hbm, inn), (mask_hbm, mask), (hub_hbm, hub.at[pl.ds(0, LEVELS)]), (fold_hbm, fold),
    ]
    loads = [pltpu.make_async_copy(src, dst, load_sem.at[i]) for i, (src, dst) in enumerate(loads)]
    for load in loads:
        load.start()

    barrier = pltpu.get_barrier_semaphore()

    def signal(wide, level):
        pl.semaphore_signal(barrier, inc=1, device_id={"wide": wide, "lev": level}, device_id_type=MESH)

    for wide in (w, left, right):
        signal(wide, 1 - lev)

    column = lax.broadcasted_iota(jnp.int32, (8, 1024), 1)
    cell, part = column // 8, (column % 8).astype(F32) * 0.125

    def table_and_signals(n, _):
        j = lax.broadcasted_iota(jnp.int32, (8, 1024), 0) + n * 8
        both = jnp.where(cell == j, 1.0 - part, 0.0) + jnp.where((cell + 1) % WIDE == j, part, 0.0)
        table[rows_at(n * 8, 8), :] = both
        for k in range(8):
            signal((w + n * 8 + k + 1) % WIDE, lev)
        return _

    lax.fori_loop(0, 15, table_and_signals, 0)
    j = lax.broadcasted_iota(jnp.int32, (8, 1024), 0) + 120
    table[120:128] = jnp.where(cell == j, 1.0 - part, 0.0) + jnp.where((cell + 1) % WIDE == j, part, 0.0)
    for k in range(7):
        signal((w + 121 + k) % WIDE, lev)

    for i in range(3):
        loads[i].wait()
    r2[pl.ds(0, 128, stride=2), :] = tmp[0:128]
    r2[pl.ds(1, 128, stride=2), :] = jnp.concatenate([tmp[1:128], tmp[127:128]], axis=0)
    columns_done = jnp.dot(mc[...], cf[...], precision=PRECISE, preferred_element_type=F32)
    win[...] = jnp.dot(r2[...], columns_done, precision=PRECISE, preferred_element_type=F32)

    near, next_near = 3 * (1 - lev), 2 - lev

    def pack_rows(nat, out, at):
        def row(level, r):
            return nat[pl.ds(own0 + level * 64 + r, 8, stride=8), :]

        for k in range(STEPS):
            for l in range(LEVELS):
                out[pl.ds(at + (k * LEVELS + l) * 8, 8), :] = row(l, 5 + k)
                out[pl.ds(at + DOWN_SIZE + (k * LEVELS + l) * 8, 8), :] = row(l, k)
        for k, (level, r) in enumerate(((near, 7), (near, 6), (next_near, 7), (near, 0), (near, 1), (next_near, 0))):
            out[pl.ds(at + 2 * DOWN_SIZE + k * 8, 8), :] = row(level, r)

    def unpack_rows(got, at, out, change):
        def put(r, level, value):
            out[pl.ds(r * 64 + level, 8, stride=8), :] = change(value)

        for k in range(STEPS):
            for l in range(LEVELS):
                put(k, lev * LEVELS + l, got[pl.ds(at + (k * LEVELS + l) * 8, 8), :])
                put(11 + k, lev * LEVELS + l, got[pl.ds(at + DOWN_SIZE + (k * LEVELS + l) * 8, 8), :])
        theirs, theirs_next = 4 - lev, 5 - 3 * lev
        for k, (r, level) in enumerate(
            ((2, theirs), (1, theirs), (2, theirs_next), (11, theirs), (12, theirs), (11, theirs_next))
        ):
            put(r, level, got[pl.ds(at + 2 * DOWN_SIZE + k * 8, 8), :])

    def row_copies(out, got, at, i):
        parts = (
            (right, lev, 0, DOWN_SIZE), (left, lev, DOWN_SIZE, DOWN_SIZE),
            (right, 1 - lev, 2 * DOWN_SIZE, 24), (left, 1 - lev, 2 * DOWN_SIZE + 24, 24),
        )
        return [
            remote(
                out.at[pl.ds(at + start, size)], got.at[pl.ds(at + start, size)],
                row_send.at[i + k], row_recv.at[i + k], wide=wide, level=level,
            )
            for k, (wide, level, start, size) in enumerate(parts)
        ]

    seen = pl.ds(pl.multiple_of(64 + 192 * lev, 64), 192)
    unseen = pl.ds(pl.multiple_of(448 * (1 - lev), 64), 64)
    lev_copies = [
        remote(nat.at[seen], nat.at[seen], lev_send.at[i], lev_recv.at[i], level=1 - lev)
        for i, nat in enumerate((nat_s, nat_k, nat_w))
    ]
    static_rows = row_copies(pack, from_rows, 0, 0) + row_copies(pack, from_rows, PACKED, 4)
    weighted_rows = row_copies(pack_w, from_rows_w, 0, 8)
    for i in (3, 4):
        loads[i].wait()

    pl.semaphore_wait(barrier, WIDE + 2)
    lev_copies[0].start()
    lev_copies[1].start()

    def near_first(n):
        a = n + (n // 2) * (5 - 2 * n)
        return a, 8 - a - 4 * ((3 - n) // 3)

    def send_window(n, _):
        a, b = near_first((WIDE - 1 - n) // (2 * GROUP))
        i = a + (b - a) * (n % 2)
        to = ((group + i) % GROUPS) * GROUP + (place + (n // 2) % GROUP) % GROUP
        remote(win.at[pl.ds(2 * to, 2)], ext.at[pl.ds(2 * w, 2)], fwd_send, fwd_recv.at[i], wide=to).start()
        return _

    own = WIDE - 2 * GROUP
    lax.fori_loop(0, own, send_window, 0)
    lax.fori_loop(own + 1, WIDE, send_window, 0)
    pltpu.make_async_copy(win.at[pl.ds(2 * w, 2)], ext.at[pl.ds(2 * w, 2)], fwd_recv.at[0]).start()

    pack_rows(nat_s, pack, 0)
    pack_rows(nat_k, pack, PACKED)
    for copy in static_rows:
        copy.start()
    weights = table[...].astype(BF16)
    ww[0:128] = weights
    ww[128:256] = weights
    wt[...] = table[...].T.astype(BF16)
    for nat in (nat_s, nat_k, nat_w):
        nat[unseen, :] = jnp.zeros((64, 128), F32)
    for rows in (v_s, v_w, kap):
        rows[0:HALO] = jnp.zeros((HALO, 128), F32)
        rows[11 * 64 : ALL_ROWS] = jnp.zeros((HALO, 128), F32)

    def to_rows(nat, out, change):
        def body(r, _):
            for t in range(TILES):
                out[rows_at((r + STEPS) * 64 + t * 8, 8), :] = change(nat[rows_at(t * 8 + r, 8, 64), :])
            return _

        lax.fori_loop(0, 8, body, 0)

    def to_natural(rows, out):
        def body(r, _):
            for t in range(TILES):
                out[rows_at(t * 8 + r, 8, 64), :] = rows[rows_at((r + STEPS) * 64 + t * 8, 8), :]
            return _

        lax.fori_loop(0, 8, body, 0)

    sublane = lax.broadcasted_iota(jnp.int32, (8, 8, 128), 1)
    lane = lax.broadcasted_iota(jnp.int32, (64, 128), 1)

    def fold_row(s_buf):
        def body(t, _):
            entry = jnp.broadcast_to(fold[pl.ds(t, 1), :], (8, 128))
            at, tile = entry % 128, entry // 128
            total = jnp.zeros((8, 128), F32)
            for u in range(TILES):
                there = jnp.take_along_axis(
                    s_buf[pl.ds(10 * 64 + u * 8, 8), :], at, axis=1, mode="promise_in_bounds"
                )
                total = jnp.where(tile == u, there, total)
            s_buf[rows_at(11 * 64 + t * 8, 8), :] = total
            return _

        @pl.when(w == WIDE - 1)
        def _():
            lax.fori_loop(0, TILES, body, 0, unroll=4)

    def diffuse(v):
        def scale_row(i, _):
            here = rows_at(i * 64, 64)
            s_a[here, :] = kap[here, :] * v[here, :]
            return _

        lax.fori_loop(0, 14, scale_row, 0, unroll=2)
        for step in range(1, STEPS + 1):
            s_buf, s_next = (s_a, s_b) if step % 2 else (s_b, s_a)
            fold_row(s_buf)

            def update_row(i, _):
                here = rows_at(i * 64, 64)
                s = s_buf[here, :]
                after = pltpu.roll(s, 1, 1)
                before = pltpu.roll(s, 127, 1)
                west = jnp.where(lane == 0, jnp.concatenate([after[56:], after[:56]], axis=0), after)
                east = jnp.where(lane == 127, jnp.concatenate([before[8:], before[:8]], axis=0), before)
                s3 = s.reshape(8, 8, 128)
                below = jnp.where(sublane == 0, 0.0, pltpu.roll(s3, 1, 1)).reshape(64, 128)
                above = jnp.where(sublane == 7, 0.0, pltpu.roll(s3, 7, 1)).reshape(64, 128)
                across = s_buf[rows_at(i * 64 + 64, 64), :] + s_buf[rows_at(i * 64 - 64, 64), :] + west + east
                new = v[here, :] + kap[here, :] * (across + 0.5 * (below + above) - 5.0 * s)
                v[here, :] = new
                if step < STEPS:
                    s_next[here, :] = kap[here, :] * new
                return _

            lax.fori_loop(step, 14 - step, update_row, 0, unroll=4)

    eighth = lax.broadcasted_iota(jnp.int32, (8, 1024), 0).astype(F32) * 0.125
    loads[5].wait()
    ens[...] = jnp.zeros((LEVELS, 8, 1024), F32)

    def ensemble_pair(n, _):
        firsts = []
        for i in near_first(n):
            wait_bytes(ext.at[pl.ds(0, 2 * GROUP)], fwd_recv.at[i])
            firsts.append(((group + GROUPS - i) % GROUPS) * GROUP)
        coarse = jnp.concatenate([ext[rows_at(2 * first, 2 * GROUP), :] for first in firsts], axis=0)
        high = coarse.astype(BF16)
        low = (coarse - high.astype(F32)).astype(BF16)
        fbuf[0 : 4 * GROUP] = jnp.dot(
            jnp.concatenate([high, low], axis=1), ww[...], preferred_element_type=F32
        )
        total = tuple(ens[l] for l in range(LEVELS))
        for k, first in enumerate(firsts):

            def member(mm, total):
                at = 2 * GROUP * k + 2 * mm
                row = jnp.broadcast_to(fbuf[pl.ds(at, 1), :], (8, 1024))
                after = jnp.broadcast_to(fbuf[pl.ds(at + 1, 1), :], (8, 1024))
                fine = row + (after - row) * eighth
                return tuple(total[l] + fine * pert[first + mm, l].astype(F32) for l in range(LEVELS))

            total = lax.fori_loop(0, GROUP, member, total, unroll=2)
        for l in range(LEVELS):
            ens[l] = total[l]
        return _

    lax.fori_loop(0, BEFORE, ensemble_pair, 0)

    for copy in lev_copies[:2] + static_rows:
        copy.wait_recv()
    to_rows(nat_s, v_s, lambda value: value)
    to_rows(nat_k, kap, jnp.sqrt)
    unpack_rows(from_rows, 0, v_s, lambda value: value)
    unpack_rows(from_rows, PACKED, kap, jnp.sqrt)
    loads[9].wait()
    kap[0:HALO] = jnp.where(w == 0, 0.0, kap[0:HALO])
    kap[11 * 64 : ALL_ROWS] = jnp.where(w == WIDE - 1, 0.0, kap[11 * 64 : ALL_ROWS])
    diffuse(v_s)
    to_natural(v_s, tmp)
    lax.fori_loop(BEFORE, 4, ensemble_pair, 0)

    for i in (6, 7, 8):
        loads[i].wait()
    j = lax.broadcasted_iota(jnp.int32, (WIDE, 1024), 0)
    x = lax.broadcasted_iota(jnp.int32, (WIDE, 1024), 1)
    spread = jnp.where(x // 8 == j, 1.0, 0.0).astype(BF16)
    blocks = jnp.concatenate([jnp.where(hub[0:LEVELS] == 1, 1.0, 0.0), jnp.zeros((12, 128), F32)], axis=0).astype(BF16)
    hubx[...] = jnp.dot(blocks, spread, preferred_element_type=F32)
    for t in range(TILES):
        columns = slice(t * 128, t * 128 + 128)
        ocean = mask[t * 8 : t * 8 + 8].astype(F32)
        for l in range(LEVELS):
            at = (l * TILES + t) * 8
            there = rows_at(own0 + at, 8)
            inc = ocean * (SCALE * ens[l, :, columns] + tmp[there, :])
            incb[at : at + 8] = inc
            misfit = inc - inn[at : at + 8]
            is_huber = jnp.broadcast_to(hubx[l : l + 1, columns], (8, 128)) > 0.5
            weight = jnp.where(is_huber, 1.0 / jnp.maximum(jnp.abs(misfit), 1.0), 1.0)
            weighted = ocean * weight * misfit
            nat_w[there, :] = weighted
            wsc[l, :, columns] = weighted * SCALE
    lev_copies[2].start()
    pack_rows(nat_w, pack_w, 0)
    for copy in weighted_rows:
        copy.start()
    inc_out = pltpu.make_async_copy(incb, inc_hbm, out_sem.at[0])
    inc_out.start()

    def adjoint_pair(n, offsets, late):
        firsts = [((group + i) % GROUPS) * GROUP for i in offsets]
        for k, first in enumerate(firsts):

            def member(mm, _):
                total = pert[first + mm, 0].astype(F32) * wsc[0]
                for l in range(1, LEVELS):
                    total = total + pert[first + mm, l].astype(F32) * wsc[l]
                fbuf[rows_at((GROUP * k + mm) * 8, 8), :] = total
                return _

            lax.fori_loop(0, GROUP, member, 0, unroll=2)
        terms = fbuf[...]
        high = terms.astype(BF16)
        parts[0:256] = high
        parts[256:512] = (terms - high.astype(F32)).astype(BF16)
        columns_done = jnp.dot(parts[...], wt[...], preferred_element_type=F32)
        gbuf[...] = columns_done[0:256] + columns_done[256:512]
        below = gbuf[pl.ds(0, 2 * GROUP, stride=8), :]
        above = jnp.zeros((2 * GROUP, 128), F32)
        for r in range(1, 8):
            row = gbuf[pl.ds(r, 2 * GROUP, stride=8), :]
            below = below + row * (1.0 - r * 0.125)
            above = above + row * (r * 0.125)
        for k, first in enumerate(firsts):
            sb[pl.ds(2 * first, GROUP, stride=2), :] = below[k * GROUP : (k + 1) * GROUP]
            sb[pl.ds(2 * first + 1, GROUP, stride=2), :] = above[k * GROUP : (k + 1) * GROUP]

            def send(p, _):
                member_at = first + (place + p) % GROUP
                source = sb.at[pl.ds(2 * member_at, 2)]
                if late:
                    slot = bb_late.at[pl.ds(2 * (LATE_TILES * lev + (2 * n - 2 * EARLY + k) * GROUP + place), 2)]
                    remote(source, slot, bwd_send, bwd_recv.at[1], wide=member_at, level=1 - lev).start()
                else:
                    slot = bb.at[pl.ds(2 * ((2 * n + k) * GROUP + place), 2)]
                remote(source, slot, bwd_send, bwd_recv.at[1 if late else 0], wide=member_at).start()
                return _

            lax.fori_loop(1 if late and offsets[k] == 0 else 0, GROUP, send, 0)

    def adjoint_far(n, _):
        a = 2 - n + 3 * (n // 2)
        adjoint_pair(n, (a, 8 - a), False)
        return _

    lax.fori_loop(0, EARLY, adjoint_far, 0)
    for n in range(EARLY, 4):
        adjoint_pair(n, PAIRS[n], True)
    mine = pl.ds(2 * w, 2)
    slot = pl.ds(2 * (LATE_TILES * lev + (7 - 2 * EARLY) * GROUP + place), 2)
    remote(sb.at[mine], bb_late.at[slot], bwd_send, bwd_recv.at[1], level=1 - lev).start()
    pltpu.make_async_copy(sb.at[mine], bb_late.at[slot], bwd_recv.at[1]).start()

    def weighted_diffusion():
        for copy in [lev_copies[2]] + weighted_rows:
            copy.wait_recv()
        to_rows(nat_w, v_w, lambda value: value)
        unpack_rows(from_rows_w, 0, v_w, lambda value: value)
        diffuse(v_w)
        to_natural(v_w, tmp)
        sgb[...] = nat_s[pl.ds(own0, OWN), :] + tmp[pl.ds(own0, OWN), :]

    def rows_adjoint(terms, offsets):
        blocks = [r2[rows_at(((group + GROUPS - i) % GROUPS) * 2 * GROUP, 2 * GROUP), :] for i in offsets]
        return lax.dot_general(
            jnp.concatenate(blocks, axis=0), terms, (((0,), (0,)), ((), ())),
            precision=PRECISE, preferred_element_type=F32,
        )

    def half_gradient():
        wait_bytes(bb, bwd_recv.at[0])
        half[...] = rows_adjoint(bb[...], [i for pair in PAIRS[:EARLY] for i in pair])
        half_copy.start()

    half_copy = remote(half, twin, half_send, half_recv, level=1 - lev)
    if D_FIRST:
        weighted_diffusion()
        half_gradient()
    else:
        half_gradient()
        weighted_diffusion()
    sg_out = pltpu.make_async_copy(sgb, sg_hbm, out_sem.at[1])
    sg_out.start()

    wait_bytes(bb_late, bwd_recv.at[1])
    rows_done = half[...] + rows_adjoint(
        bb_late[0 : 2 * LATE_TILES] + bb_late[2 * LATE_TILES :], [i for pair in PAIRS[EARLY:] for i in pair]
    )
    half_copy.wait_recv()
    mgb[...] = mc[...] + lax.dot_general(
        rows_done + twin[...], cf[...], (((1,), (1,)), ((), ())), precision=PRECISE, preferred_element_type=F32
    )
    mg_out = pltpu.make_async_copy(mgb, mg_hbm, out_sem.at[2])
    mg_out.start()

    wait_bytes(ext.at[pl.ds(0, 254)], fwd_send)
    wait_bytes(nat_s.at[pl.ds(0, 2 * (WIDE + LATE_TILES) - 2)], bwd_send)
    for copy in lev_copies + static_rows + weighted_rows + [half_copy]:
        copy.wait_send()
    inc_out.wait()
    sg_out.wait()
    mg_out.wait()


def finish(*refs):
    sources, results, held, sem = refs[:3], refs[3:6], refs[6:9], refs[9]
    inward = [pltpu.make_async_copy(a, b, sem.at[0, i]) for i, (a, b) in enumerate(zip(sources, held))]
    outward = [pltpu.make_async_copy(a, b, sem.at[1, i]) for i, (a, b) in enumerate(zip(held, results))]
    for copy in inward:
        copy.start()
    for into, out in zip(inward, outward):
        into.wait()
        out.start()
    for copy in outward:
        copy.wait()


def natural(array):
    levels = array.shape[0]
    return array.reshape(levels, 8, TILES, 128).transpose(0, 2, 1, 3).reshape(levels * 64, 128)


def from_natural(array):
    return array.reshape(LEVELS, TILES, 8, 128).transpose(0, 2, 1, 3).reshape(LEVELS, 8, 1024)


def on_device(
    member_control, static_control, perturbations, innovation, diffusivity,
    rows_factor, column_factor, ocean_mask, huber_blocks, fold_map,
):
    hbm = pl.BlockSpec(memory_space=pltpu.HBM)
    dma = pltpu.SemaphoreType.DMA

    def vmem(*shape, dtype=F32):
        return pltpu.VMEM(shape, dtype)

    increment, member_gradient, static_gradient = pl.pallas_call(
        kernel,
        out_shape=(
            jax.ShapeDtypeStruct((OWN, 128), F32),
            jax.ShapeDtypeStruct((128, 128), F32),
            jax.ShapeDtypeStruct((OWN, 128), F32),
        ),
        in_specs=[hbm] * 10,
        out_specs=[hbm] * 3,
        scratch_shapes=[
            vmem(WIDE, LEVELS, 8, 1024, dtype=BF16),
            vmem(128, 128), vmem(128, 128), vmem(256, 128),
            vmem(256, 128), vmem(256, 128), vmem(64 * EARLY, 128), vmem(256, 128),
            vmem(512, 128), vmem(512, 128), vmem(512, 128),
            vmem(OWN, 128), vmem(64, 128, dtype=jnp.int32), vmem(8, 128, dtype=jnp.int32),
            vmem(8, 128, dtype=jnp.int32),
            vmem(ALL_ROWS, 128), vmem(ALL_ROWS, 128), vmem(ALL_ROWS, 128),
            vmem(ALL_ROWS, 128), vmem(ALL_ROWS, 128),
            vmem(512, 128),
            vmem(256, 1024, dtype=BF16), vmem(1024, 128, dtype=BF16),
            vmem(512, 1024, dtype=BF16), vmem(256, 1024), vmem(256, 128),
            vmem(LEVELS, 8, 1024), vmem(LEVELS, 8, 1024), vmem(16, 1024),
            vmem(OWN, 128), vmem(OWN, 128), vmem(128, 128),
            vmem(2 * PACKED, 128), vmem(PACKED, 128), vmem(2 * PACKED, 128), vmem(PACKED, 128),
            vmem(128, 128), vmem(128, 128), vmem(WIDE, 1024), vmem(4 * LATE_TILES, 128),
            dma((10,)), dma((3,)), dma, dma((8,)), dma, dma((2,)), dma((3,)), dma((3,)), dma((12,)), dma((12,)), dma, dma,
        ],
        compiler_params=pltpu.CompilerParams(
            collective_id=0, has_side_effects=True, vmem_limit_bytes=63 << 20
        ),
        name="increment_and_gradients",
    )(
        member_control.reshape(128, 128),
        natural(static_control),
        perturbations,
        natural(innovation),
        natural(diffusivity),
        rows_factor,
        column_factor,
        natural(ocean_mask[None]),
        huber_blocks.reshape(LEVELS, 128),
        fold_map.reshape(8, 128),
    )
    increment, member_gradient, static_gradient = pl.pallas_call(
        finish,
        out_shape=(
            jax.ShapeDtypeStruct((OWN, 128), F32),
            jax.ShapeDtypeStruct((128, 128), F32),
            jax.ShapeDtypeStruct((OWN, 128), F32),
        ),
        in_specs=[hbm] * 3,
        out_specs=[hbm] * 3,
        scratch_shapes=[vmem(OWN, 128), vmem(128, 128), vmem(OWN, 128), dma((2, 3))],
        compiler_params=pltpu.CompilerParams(vmem_limit_bytes=63 << 20),
        name="finish",
    )(increment, member_gradient, static_gradient)
    return from_natural(increment), member_gradient[None], from_natural(static_gradient)


def solution(mesh):
    return jax.shard_map(
        on_device,
        mesh=mesh,
        in_specs=(
            P("wide", None, None),
            P("lev", "wide", None),
            P(None, "lev", "wide", None),
            P("lev", "wide", None),
            P("lev", "wide", None),
            P(),
            P(),
            P("wide", None),
            P("lev", "wide", None),
            P(),
        ),
        out_specs=(P("lev", "wide", None), P("wide", None, None), P("lev", "wide", None)),
        check_vma=False,
    )
```
